256 devices in a mesh: row: 64 (over y, z, core), col: 4 (over x).
Axes of the slice: x: 4, y: 4, z: 8, core: 2. Of those that a mesh axis runs over, the one named last changes fastest.
Arguments:
- trailing: float32 [65536, 4096], P('row', 'col'), may hold values from -6 to 6
- panel_y: float32 [65536, 256], P(('row', 'col')), may hold values from -0.1875 to 0.1875
- panel_t: float32 [16384, 256], P('row'), may hold values from 0.5 to 1.5
- tree_v: float32 [3, 16384, 256], P(None, 'row'), may hold values from -0.375 to 0.375, as said below
- tree_t: float32 [3, 16384, 256], P(None, 'row'), may hold values from 0.5 to 1.5, as said below
Outputs:
- updated: float32 [65536, 4096], P('row', 'col')
The draws below stay inside these ranges and needn't reach their ends.
Inputs may be any that keep to these rules, and one draw needn't show every extreme that they name: For each level l, the blocks of 256 rows that tree_v[l] holds for two tile rows that differ only in bit l are equal. For each level l, the blocks of 256 rows that tree_t[l] holds for two tile rows that differ only in bit l are equal.
All inputs are finite; a program needn't handle non-finite values.
Results may differ from the reference program's by a relative error of at most 0.0001.
Values sent between devices are 32-bit elements; how exact they have to be, the bound alone decides.
No kernel may reach another device: no remote copies, remote signals or barrier semaphores. Data moves between devices by JAX's collectives and lax.ppermute only.
A program may use at most 64 MiB of HBM per device.

```python
import math
import jax
import jax.numpy as jnp
from jax import lax

B = 256
M_DEV = 1024
LEVELS = 3
M = 65536
N = 4096
N_ROW = 64


def pair_copy(base):
    levels = []
    for level in range(LEVELS):
        leads = jnp.arange(N_ROW) & ~(1 << level)
        levels.append(base[level][leads])
    return jnp.stack(levels).reshape(LEVELS, N_ROW * B, B)


def draw_tree_v(key, part):
    base = jax.random.normal(key, (LEVELS, N_ROW, B, B), jnp.float32) * (1.0 / math.sqrt(B))
    base = jnp.clip(base, -0.375, 0.375)
    return pair_copy(base)


def draw_tree_t(key, part):
    base = jax.random.uniform(key, (LEVELS, N_ROW, B, B), jnp.float32, 0.5, 1.5)
    return pair_copy(base)


def level_of(key, extent, cuts, low, largest):
    gain, own = 1.0, jax.random.fold_in(key, 6)
    for position, shards_of in cuts:
        heights = jnp.exp(jax.random.uniform(jax.random.fold_in(own, position), (shards_of,), jnp.float32, low / len(cuts), largest / len(cuts)))
        gain = gain * jnp.repeat(heights, extent[position] // shards_of).reshape([-1 if axis == position else 1 for axis in range(len(extent))])
    return gain


def centred(stream_key, dims, scale, reach, shards=(), kind=jnp.bfloat16):
    drawn = scale * jax.random.normal(stream_key, dims, jnp.float32)
    if shards:
        drawn = drawn * level_of(stream_key, dims, shards, -0.22, 0.18)
    return jnp.clip(drawn, -reach, reach).astype(kind)


def setup_inputs(seed: int = 0) -> dict:
    arg_keys = jax.random.split(jax.random.key(seed), 6)
    return {
        "trailing": centred(arg_keys[0], (M, N), 1.0, 6.0, ((0, 64), (1, 4)), jnp.float32),
        "panel_y": centred(arg_keys[1], (M, B), M_DEV ** -0.5, 0.1875, ((0, 256),), jnp.float32),
        "panel_t": jnp.clip(0.5 + 1.0 * jax.random.uniform(arg_keys[2], (N_ROW * B, B), jnp.float32) ** level_of(arg_keys[2], (N_ROW * B, B), ((0, 64),), -0.2, 0.2), 0.5, 1.5),
        "tree_v": draw_tree_v(jax.random.fold_in(arg_keys[5], 71), 0),
        "tree_t": draw_tree_t(jax.random.fold_in(arg_keys[5], 71), 0),
    }


def unit_lower(values):
    rows = jnp.arange(values.shape[-2])[:, None]
    cols = jnp.arange(values.shape[-1])[None, :]
    return jnp.where(rows > cols, values, jnp.where(rows == cols, jnp.float32(1.0), jnp.float32(0.0)))

def triangle_factor(values):
    width = values.shape[-1]
    rows = jnp.arange(width)[:, None]
    cols = jnp.arange(width)[None, :]
    scale = 2.0 / math.sqrt(width)
    return jnp.where(rows == cols, values, jnp.where(cols > rows, (values - 1.0) * scale, jnp.float32(0.0)))

def upper_part(values):
    width = values.shape[-1]
    rows = jnp.arange(width)[:, None]
    cols = jnp.arange(width)[None, :]
    return jnp.where(cols >= rows, values, jnp.float32(0.0))

def reference(trailing, panel_y, panel_t, tree_v, tree_t):
    highest = lax.Precision.HIGHEST
    blocks = trailing.reshape(N_ROW, M_DEV, N)
    reflect = panel_y.reshape(N_ROW, M_DEV, B)
    factors = panel_t.reshape(N_ROW, B, B)

    def local_update(pieces):
        block, vectors, tri = pieces
        lower = unit_lower(vectors)
        proj = jnp.einsum('mb,mn->bn', lower, block, precision=highest)
        weight = jnp.einsum('kb,kn->bn', triangle_factor(tri), proj, precision=highest)
        return block - jnp.einsum('mb,bn->mn', lower, weight, precision=highest)
    local = lax.map(local_update, (blocks, reflect, factors))
    tops = local[:, :B, :]
    for level in range(LEVELS):
        span = 1 << level
        groups = N_ROW // (2 * span)
        paired = tops.reshape(groups, 2, span, B, N)
        first = paired[:, 0]
        second = paired[:, 1]
        vees = upper_part(tree_v[level].reshape(groups, 2, span, B, B)[:, 0])
        tees = triangle_factor(tree_t[level].reshape(groups, 2, span, B, B)[:, 0])
        summed = first + jnp.einsum('gskb,gskn->gsbn', vees, second, precision=highest)
        weight = jnp.einsum('gskb,gskn->gsbn', tees, summed, precision=highest)
        new_first = first - weight
        new_second = second - jnp.einsum('gsbk,gskn->gsbn', vees, weight, precision=highest)
        tops = jnp.stack([new_first, new_second], axis=1).reshape(N_ROW, B, N)
    local = local.at[:, :B, :].set(tops)
    return local.reshape(M, N)
```

```python
import functools
import math

import jax
import jax.numpy as jnp
from jax import lax
from jax.experimental import pallas as pl
from jax.experimental.pallas import tpu as pltpu
from jax.sharding import PartitionSpec as P


WIDTHS = (256, 256, 256, 256)
F32 = jnp.float32
BF16 = jnp.bfloat16
VMEM = pl.BlockSpec(memory_space=pltpu.VMEM)
SMEM = pl.BlockSpec(memory_space=pltpu.SMEM)
ANY = pl.BlockSpec(memory_space=pl.ANY)


def split(values):
    high = values.astype(BF16)
    return high, (values - high.astype(F32)).astype(BF16)


def dot3(left, right):
    mul = functools.partial(jnp.dot, preferred_element_type=F32)
    return mul(left[0], right[0]) + (mul(left[0], right[1]) + mul(left[1], right[0]))


def grids(shape):
    return lax.broadcasted_iota(jnp.int32, shape, 0), lax.broadcasted_iota(jnp.int32, shape, 1)


def unit_lower(values, first_row):
    rows, cols = grids(values.shape)
    rows = rows + first_row
    return jnp.where(rows > cols, values, jnp.where(rows == cols, F32(1.0), F32(0.0)))


def triangle_factor(values):
    rows, cols = grids(values.shape)
    scale = 2.0 / math.sqrt(values.shape[-1])
    return jnp.where(rows == cols, values, jnp.where(cols > rows, (values - 1.0) * scale, F32(0.0)))


def upper_part(values):
    rows, cols = grids(values.shape)
    return jnp.where(cols >= rows, values, F32(0.0))


def prepare_kernel(place, panel_t, tree_v, tree_t, th, tl, *mixes):
    th[...], tl[...] = split(triangle_factor(panel_t[...]).T)
    levels = tree_v.shape[0]
    width = panel_t.shape[1]
    for level in range(levels):
        high, low = mixes[2 * level], mixes[2 * level + 1]
        leads = (place[0] >> level) & 1 == 0
        vees = upper_part(tree_v[level])
        tees = split(triangle_factor(tree_t[level]).T)

        @pl.when(leads)
        def _():
            high[:, :width], low[:, :width] = tees
            high[:, width:], low[:, width:] = split(dot3(tees, split(vees.T)))

        @pl.when(jnp.logical_not(leads))
        def _():
            both = split(dot3(split(vees), tees))
            high[:, width:], low[:, width:] = both
            high[:, :width], low[:, :width] = split(dot3(both, split(vees.T)))


def early_kernel(place, own, left_a, left_b, right_a, right_b, block, partial, yh, yl):
    col = place[1]
    count = block.shape[0] // own.shape[0]
    size = own.shape[0]
    half = size // 2
    total = None
    for shift, parts in ((0, (own,)), (count - 1, (left_a, left_b)), (1, (right_a, right_b))):
        start = pl.multiple_of(lax.rem(col + shift, count) * size, size)
        rows = parts[0][...] if len(parts) == 1 else jnp.concatenate([p[...] for p in parts], axis=0)
        rows = unit_lower(rows, start)
        yh[pl.ds(start, size), :], yl[pl.ds(start, size), :] = split(rows)
        term = dot3(split(rows.T), split(block[pl.ds(start, size), :]))
        total = term if total is None else total + term
    partial[...] = total


def last_kernel(first, widths, place, partial, opp_a, opp_b, block, th, tl, yh_in, yl_in, *outs):
    col = place[1]
    size = 2 * opp_a.shape[0]
    count = block.shape[0] // size
    tops, weights, yh, yl = outs[: len(widths)], outs[len(widths) : 2 * len(widths)], outs[-2], outs[-1]
    start = pl.multiple_of(lax.rem(col + count // 2, count) * size, size)
    rows = jnp.concatenate([opp_a[...], opp_b[...]], axis=0)
    rows = unit_lower(rows, start)
    yh[...] = yh_in[...]
    yl[...] = yl_in[...]
    yh[pl.ds(start, size), :], yl[pl.ds(start, size), :] = split(rows)
    flipped = split(rows.T)
    upper = (yh[:size, :], yl[:size, :])
    factor = (th[...], tl[...])
    for k, width in enumerate(widths):
        span = slice(first, first + width)
        proj = partial[:, span] + dot3(flipped, split(block[pl.ds(start, size), span]))
        weight = dot3(factor, split(proj))
        weights[k][...] = weight
        tops[k][...] = block[:size, span] - dot3(upper, split(weight))
        first += width


def rest_kernel(block, yh, yl, *args):
    weights, out = args[:-1], args[-1]
    first = 0
    for weight in weights:
        span = slice(first, first + weight.shape[1])
        out[:, span] = block[:, span] - dot3((yh[...], yl[...]), split(weight[...]))
        first += weight.shape[1]


def mixed(mine, theirs, high, low):
    width = mine.shape[0]
    one = dot3((high[:, :width], low[:, :width]), split(mine[...]))
    two = dot3((high[:, width:], low[:, width:]), split(theirs[...]))
    return mine[...] - (one + two)


def level_kernel(mine, theirs, high, low, out):
    out[...] = mixed(mine, theirs, high, low)


def final_kernel(mine, theirs, high, low, whole, out):
    out[...] = mixed(mine, theirs, high, low)


def params(mib):
    return pltpu.CompilerParams(vmem_limit_bytes=mib << 20)


def shaped(shape, dtype=F32):
    return jax.ShapeDtypeStruct(shape, dtype)


def cost(flops, moved):
    return pl.CostEstimate(flops=flops, bytes_accessed=moved, transcendentals=0)


def per_device(trailing, panel_y, panel_t, tree_v, tree_t):
    size, width = panel_y.shape
    rows, columns = trailing.shape
    levels = tree_v.shape[0]
    half = size // 2
    count = lax.axis_size("col")
    place = jnp.stack([lax.axis_index("row"), lax.axis_index("col")]).astype(jnp.int32)
    onward = [(c, (c + 1) % count) for c in range(count)]
    backward = [(c, (c - 1) % count) for c in range(count)]

    own_a, own_b = panel_y[:half], panel_y[half:]
    left_a = lax.ppermute(own_a, "col", onward)
    right_b = lax.ppermute(own_b, "col", backward)
    left_b = lax.ppermute(own_b, "col", onward)
    right_a = lax.ppermute(own_a, "col", backward)
    opp_a = lax.ppermute(left_a, "col", onward)
    opp_b = lax.ppermute(right_b, "col", backward)

    mix = shaped((width, 2 * width), BF16)
    th, tl, *mixes = pl.pallas_call(
        prepare_kernel,
        out_shape=[shaped((width, width), BF16)] * 2 + [mix] * (2 * levels),
        in_specs=[SMEM, VMEM, VMEM, VMEM],
        out_specs=[VMEM] * (2 + 2 * levels),
        compiler_params=params(16),
        cost_estimate=cost(2 * 3 * 3 * levels * width**3, 1 << 20),
        name="prepare",
    )(place, panel_t, tree_v, tree_t)

    flops = 2 * 3 * size * width * columns
    partial, yh, yl = pl.pallas_call(
        early_kernel,
        out_shape=[shaped((width, columns)), shaped((rows, width), BF16), shaped((rows, width), BF16)],
        in_specs=[SMEM] + [VMEM] * 6,
        out_specs=[VMEM] * 3,
        compiler_params=params(20),
        cost_estimate=cost(3 * flops, 4 << 20),
        name="early",
    )(place, panel_y, left_a, left_b, right_a, right_b, trailing)

    tops, weights = [], []
    first = 0
    for part in (WIDTHS[:1], WIDTHS[1:]):
        n = len(part)
        got = pl.pallas_call(
            functools.partial(last_kernel, first, part),
            out_shape=[shaped((width, w)) for w in part] * 2 + [shaped((rows, width), BF16)] * 2,
            in_specs=[SMEM] + [VMEM] * 8,
            out_specs=[VMEM] * (2 * n + 2),
            compiler_params=params(20),
            input_output_aliases={7: 2 * n, 8: 2 * n + 1},
            cost_estimate=cost(3 * flops * sum(part) // columns, 2 << 20),
            name="last",
        )(place, partial, opp_a, opp_b, trailing, th, tl, yh, yl)
        tops += got[:n]
        weights += got[n : 2 * n]
        yh, yl = got[-2:]
        first += sum(part)

    out = pl.pallas_call(
        rest_kernel,
        grid=(rows // size - 1,),
        out_shape=shaped((rows, columns)),
        in_specs=[
            pl.BlockSpec((size, columns), lambda i: (i + 1, 0)),
            pl.BlockSpec((size, width), lambda i: (i + 1, 0)),
            pl.BlockSpec((size, width), lambda i: (i + 1, 0)),
        ]
        + [pl.BlockSpec((width, w), lambda i: (0, 0)) for w in WIDTHS],
        out_specs=pl.BlockSpec((size, columns), lambda i: (i + 1, 0)),
        compiler_params=params(20),
        cost_estimate=cost(3 * flops, 8 << 20),
        name="rest",
    )(trailing, yh, yl, *weights)

    for level in range(levels):
        route = [(r, r ^ (1 << level)) for r in range(lax.axis_size("row"))]
        high, low = mixes[2 * level], mixes[2 * level + 1]
        first = 0
        for k, w in enumerate(WIDTHS):
            theirs = lax.ppermute(tops[k], "row", route)
            estimate = cost(2 * 3 * 2 * width * width * w, 1 << 20)
            if level < levels - 1:
                tops[k] = pl.pallas_call(
                    level_kernel,
                    out_shape=shaped((width, w)),
                    in_specs=[VMEM] * 4,
                    out_specs=VMEM,
                    compiler_params=params(8),
                    cost_estimate=estimate,
                    name="level",
                )(tops[k], theirs, high, low)
            else:
                spot = first // w
                out = pl.pallas_call(
                    final_kernel,
                    grid=(1,),
                    out_shape=shaped((rows, columns)),
                    in_specs=[
                        pl.BlockSpec((width, w), lambda i: (0, 0)),
                        pl.BlockSpec((width, w), lambda i: (0, 0)),
                        pl.BlockSpec((width, 2 * width), lambda i: (0, 0)),
                        pl.BlockSpec((width, 2 * width), lambda i: (0, 0)),
                        ANY,
                    ],
                    out_specs=pl.BlockSpec((width, w), lambda i, spot=spot: (0, spot)),
                    compiler_params=params(8),
                    input_output_aliases={4: 0},
                    cost_estimate=estimate,
                    name="final",
                )(tops[k], theirs, high, low, out)
            first += w
    return out


def solution(mesh):
    placed = (
        P("row", "col"),
        P(("row", "col"), None),
        P("row", None),
        P(None, "row", None),
        P(None, "row", None),
    )
    return jax.shard_map(
        per_device, mesh=mesh, in_specs=placed, out_specs=P("row", "col"), check_vma=False
    )
```

```python
import functools
import math

import jax
import jax.numpy as jnp
from jax import lax
from jax.experimental import pallas as pl
from jax.experimental.pallas import tpu as pltpu
from jax.sharding import PartitionSpec as P


WIDTHS = (128, 128, 256, 256, 256)
F32 = jnp.float32
BF16 = jnp.bfloat16
VMEM = pl.BlockSpec(memory_space=pltpu.VMEM)
SMEM = pl.BlockSpec(memory_space=pltpu.SMEM)
HBM = pl.BlockSpec(memory_space=pltpu.HBM)
ANY = pl.BlockSpec(memory_space=pl.ANY)


def split(values):
    high = values.astype(BF16)
    return high, (values - high.astype(F32)).astype(BF16)


def dot3(left, right):
    mul = functools.partial(jnp.dot, preferred_element_type=F32)
    return mul(left[0], right[0]) + (mul(left[0], right[1]) + mul(left[1], right[0]))


def grids(shape):
    return lax.broadcasted_iota(jnp.int32, shape, 0), lax.broadcasted_iota(jnp.int32, shape, 1)


def unit_lower(values, first_row):
    rows, cols = grids(values.shape)
    rows = rows + first_row
    return jnp.where(rows > cols, values, jnp.where(rows == cols, F32(1.0), F32(0.0)))


def triangle_factor(values):
    rows, cols = grids(values.shape)
    scale = 2.0 / math.sqrt(values.shape[-1])
    return jnp.where(rows == cols, values, jnp.where(cols > rows, (values - 1.0) * scale, F32(0.0)))


def upper_part(values):
    rows, cols = grids(values.shape)
    return jnp.where(cols >= rows, values, F32(0.0))


def mix_level(leads, tree_v, tree_t, high, low):
    width = tree_v.shape[0]
    vees = upper_part(tree_v)
    tees = split(triangle_factor(tree_t).T)

    @pl.when(leads)
    def _():
        high[:, :width], low[:, :width] = tees
        high[:, width:], low[:, width:] = split(dot3(tees, split(vees.T)))

    @pl.when(jnp.logical_not(leads))
    def _():
        both = split(dot3(split(vees), tees))
        high[:, width:], low[:, width:] = both
        high[:, :width], low[:, :width] = split(dot3(both, split(vees.T)))


def start_all(pairs, sems):
    copies = [pltpu.make_async_copy(a, b, sems.at[i]) for i, (a, b) in enumerate(pairs)]
    for copy in copies:
        copy.start()
    return copies


def prepare_kernel(place, panel_t, tree_v, tree_t, trailing, th, tl, high, low, block, tri, vee, tee, sems):
    piece = trailing.at[:, : block.shape[1]]
    copies = start_all(((panel_t, tri), (tree_v.at[0], vee), (tree_t.at[0], tee), (piece, block)), sems)
    copies[0].wait()
    th[...], tl[...] = split(triangle_factor(tri[...]).T)
    copies[1].wait()
    copies[2].wait()
    mix_level(place[0] & 1 == 0, vee[...], tee[...], high, low)
    copies[3].wait()


def mixes_kernel(place, tree_v, tree_t, trailing, after, *args):
    del after
    levels = tree_v.shape[0]
    mixes, block, (vee, tee, sems) = args[:-4], args[-4], args[-3:]
    pairs = []
    for level in range(1, levels):
        pairs += [(tree_v.at[level], vee.at[level - 1]), (tree_t.at[level], tee.at[level - 1])]
    pairs.append((trailing.at[:, trailing.shape[1] - block.shape[1] :], block))
    copies = start_all(pairs, sems)
    for level in range(1, levels):
        copies[2 * level - 2].wait()
        copies[2 * level - 1].wait()
        mix_level((place[0] >> level) & 1 == 0, vee[level - 1], tee[level - 1], *mixes[2 * level - 2 : 2 * level])
    copies[-1].wait()


def opposite_rows(col, size, count):
    return pl.multiple_of(lax.rem(col + count // 2, count) * size, size)


def keep(rows, start, yh, yl, fh, fl):
    here = pl.ds(start, rows.shape[0])
    rows = unit_lower(rows, start)
    flipped = split(rows.T)
    yh[here, :], yl[here, :] = split(rows)
    fh[:, here], fl[:, here] = flipped
    return flipped


def early_kernel(place, own, left_a, left_b, right_a, right_b, block, partial, yh, yl, fh, fl):
    col = place[1]
    size = own.shape[0]
    count = block.shape[0] // size
    width = partial.shape[1]
    total = None
    for shift, parts in ((0, (own,)), (count - 1, (left_a, left_b)), (1, (right_a, right_b))):
        start = pl.multiple_of(lax.rem(col + shift, count) * size, size)
        rows = parts[0][...] if len(parts) == 1 else jnp.concatenate([p[...] for p in parts], axis=0)
        flipped = keep(rows, start, yh, yl, fh, fl)
        term = dot3(flipped, split(block[pl.ds(start, size), :width]))
        total = term if total is None else total + term
    partial[...] = total


def first_kernel(place, partial, opp_a, opp_b, block, th, tl, *args):
    top, proj, gh, gl, yh, yl, fh, fl = args[4:]
    size = 2 * opp_a.shape[0]
    width = partial.shape[1]
    start = opposite_rows(place[1], size, block.shape[0] // size)
    rows = jnp.concatenate([opp_a[...], opp_b[...]], axis=0)
    flipped = keep(rows, start, yh, yl, fh, fl)
    gain = split(dot3((yh[:size, :], yl[:size, :]), (th[...], tl[...])))
    value = partial[...] + dot3(flipped, split(block[pl.ds(start, size), :width]))
    top[...] = block[:size, :width] - dot3(gain, split(value))
    proj[...] = value
    gh[...], gl[...] = gain


def next_kernel(span, block, fh, fl, gh, gl, top, proj):
    values = block[:, span]
    value = dot3((fh[...], fl[...]), split(values))
    top[...] = values[: top.shape[0]] - dot3((gh[...], gl[...]), split(value))
    proj[...] = value


def rest_kernel(block, yh, yl, th, tl, *args):
    projs, out = args[:-1], args[-1]
    first = 0
    for proj in projs:
        span = slice(first, first + proj.shape[1])
        weight = dot3((th[...], tl[...]), split(proj[...]))
        out[:, span] = block[:, span] - dot3((yh[...], yl[...]), split(weight))
        first += proj.shape[1]


def mixed(mine, theirs, high, low):
    width = mine.shape[0]
    one = dot3((high[:, :width], low[:, :width]), split(mine[...]))
    two = dot3((high[:, width:], low[:, width:]), split(theirs[...]))
    return mine[...] - (one + two)


def level_kernel(mine, theirs, high, low, out):
    out[...] = mixed(mine, theirs, high, low)


def final_kernel(mine, theirs, high, low, whole, out):
    out[...] = mixed(mine, theirs, high, low)


def shaped(shape, dtype=F32):
    return jax.ShapeDtypeStruct(shape, dtype)


EARLY = 2


def call(kernel, **options):
    mib = options.pop("mib")
    flops, moved = options.pop("cost")
    return pl.pallas_call(
        kernel,
        compiler_params=pltpu.CompilerParams(vmem_limit_bytes=mib << 20),
        cost_estimate=pl.CostEstimate(flops=flops, bytes_accessed=moved, transcendentals=0),
        **options,
    )


def fixed(values):
    return pltpu.with_memory_space_constraint(values, pltpu.HBM)


def whole(shape):
    return pl.BlockSpec(shape, lambda i: (0, 0))


def update(trailing, panel_y, panel_t, tree_v, tree_t):
    size, width = panel_y.shape
    rows, columns = trailing.shape
    levels = tree_v.shape[0]
    half = size // 2
    count = lax.axis_size("col")
    place = jnp.stack([lax.axis_index("row"), lax.axis_index("col")]).astype(jnp.int32)
    onward = [(c, (c + 1) % count) for c in range(count)]
    backward = [(c, (c - 1) % count) for c in range(count)]

    own_a, own_b = panel_y[:half], panel_y[half:]
    left_a = lax.ppermute(own_a, "col", onward)
    right_b = lax.ppermute(own_b, "col", backward)
    left_b = lax.ppermute(own_b, "col", onward)
    right_a = lax.ppermute(own_a, "col", backward)
    opp_a = lax.ppermute(left_a, "col", onward)
    opp_b = lax.ppermute(right_b, "col", backward)

    square = shaped((width, width), BF16)
    mix = shaped((width, 2 * width), BF16)
    tall = shaped((rows, width), BF16)
    wide = shaped((width, rows), BF16)
    ahead = sum(WIDTHS[:EARLY])
    cube = 2 * 3 * width**3
    trailing = fixed(trailing)
    panel_t, tree_v, tree_t = fixed(panel_t), fixed(tree_v), fixed(tree_t)
    th, tl, high0, low0, block = call(
        prepare_kernel,
        out_shape=[square, square, mix, mix, shaped((rows, ahead))],
        in_specs=[SMEM] + [HBM] * 4,
        out_specs=[VMEM] * 5,
        scratch_shapes=[pltpu.VMEM((width, width), F32)] * 3 + [pltpu.SemaphoreType.DMA((4,))],
        mib=12,
        cost=(3 * cube, 2 << 20),
    )(place, panel_t, tree_v, tree_t, trailing)

    w = WIDTHS[0]
    partial, yh, yl, fh, fl = call(
        early_kernel,
        out_shape=[shaped((width, w)), tall, tall, wide, wide],
        in_specs=[SMEM] + [VMEM] * 6,
        out_specs=[VMEM] * 5,
        mib=12,
        cost=(2 * cube, 4 << 20),
    )(place, panel_y, left_a, left_b, right_a, right_b, block)

    top, proj, gh, gl, yh, yl, fh, fl = call(
        first_kernel,
        out_shape=[shaped((width, w))] * 2 + [square] * 2 + [tall, tall, wide, wide],
        in_specs=[SMEM] + [VMEM] * 10,
        out_specs=[VMEM] * 8,
        mib=12,
        input_output_aliases={7: 4, 8: 5, 9: 6, 10: 7},
        cost=(2 * cube, 2 << 20),
    )(place, partial, opp_a, opp_b, block, th, tl, yh, yl, fh, fl)
    tops, projs = [top], [proj]

    spans, first = [], 0
    for w in WIDTHS:
        spans.append(slice(first, first + w))
        first += w
    mixes = [(high0, low0)]
    out = None

    def exchange(level, k):
        route = [(r, r ^ (1 << level)) for r in range(lax.axis_size("row"))]
        theirs = lax.ppermute(tops[k], "row", route)
        high, low = mixes[level]
        w = WIDTHS[k]
        estimate = (2 * cube * w // width, 1 << 20)
        if level < levels - 1:
            tops[k] = call(
                level_kernel, out_shape=shaped((width, w)), in_specs=[VMEM] * 4, out_specs=VMEM, mib=8, cost=estimate
            )(tops[k], theirs, high, low)
            return out
        spot = spans[k].start // w
        return call(
            final_kernel,
            grid=(1,),
            out_shape=shaped((rows, columns)),
            in_specs=[whole((width, w)), whole((width, w)), whole((width, 2 * width)), whole((width, 2 * width)), ANY],
            out_specs=pl.BlockSpec((width, w), lambda i: (0, spot)),
            input_output_aliases={4: 0},
            mib=8,
            cost=estimate,
        )(tops[k], theirs, high, low, out)

    exchange(0, 0)
    *later, block_late = call(
        mixes_kernel,
        out_shape=[mix] * (2 * levels - 2) + [shaped((rows, columns - ahead))],
        in_specs=[SMEM] + [HBM] * 3 + [ANY],
        out_specs=[VMEM] * (2 * levels - 1),
        scratch_shapes=[pltpu.VMEM((levels - 1, width, width), F32)] * 2
        + [pltpu.SemaphoreType.DMA((2 * levels - 1,))],
        mib=16,
        cost=(2 * (levels - 1) * cube, 4 << 20),
    )(place, tree_v, tree_t, trailing, tops[0])
    mixes += [(later[2 * i], later[2 * i + 1]) for i in range(levels - 1)]

    for k in range(1, len(WIDTHS)):
        source, offset = (block, 0) if k < EARLY else (block_late, ahead)
        span = slice(spans[k].start - offset, spans[k].stop - offset)
        top, proj = call(
            functools.partial(next_kernel, span),
            out_shape=[shaped((width, WIDTHS[k]))] * 2,
            in_specs=[VMEM] * 5,
            out_specs=[VMEM] * 2,
            mib=16,
            cost=(5 * cube * WIDTHS[k] // width, 2 << 20),
        )(source, fh, fl, gh, gl)
        tops.append(top)
        projs.append(proj)
        exchange(0, k)

    out = call(
        rest_kernel,
        grid=(rows // size - 1,),
        out_shape=shaped((rows, columns)),
        in_specs=[
            pl.BlockSpec((size, columns), lambda i: (i + 1, 0)),
            pl.BlockSpec((size, width), lambda i: (i + 1, 0)),
            pl.BlockSpec((size, width), lambda i: (i + 1, 0)),
            whole((width, width)),
            whole((width, width)),
        ]
        + [whole((width, w)) for w in WIDTHS],
        out_specs=pl.BlockSpec((size, columns), lambda i: (i + 1, 0)),
        mib=20,
        cost=(20 * cube, 8 << 20),
    )(trailing, yh, yl, th, tl, *projs)

    for level in range(1, levels):
        for k in range(len(WIDTHS)):
            out = exchange(level, k)
    return out


def solution(mesh):
    placed = (
        P("row", "col"),
        P(("row", "col"), None),
        P("row", None),
        P(None, "row", None),
        P(None, "row", None),
    )
    return jax.shard_map(update, mesh=mesh, in_specs=placed, out_specs=P("row", "col"), check_vma=False)
```

```python
import functools
import math

import jax
import jax.numpy as jnp
from jax import lax
from jax.experimental import pallas as pl
from jax.experimental.pallas import tpu as pltpu
from jax.sharding import PartitionSpec as P


UNITS = ((128, 128), (128, 128), (256,), (256,))
F32 = jnp.float32
BF16 = jnp.bfloat16
VMEM = pl.BlockSpec(memory_space=pltpu.VMEM)
SMEM = pl.BlockSpec(memory_space=pltpu.SMEM)
HBM = pl.BlockSpec(memory_space=pltpu.HBM)
ANY = pl.BlockSpec(memory_space=pl.ANY)


def split(values):
    high = values.astype(BF16)
    return high, (values - high.astype(F32)).astype(BF16)


def dot3(left, right):
    mul = functools.partial(jnp.dot, preferred_element_type=F32)
    return mul(left[0], right[0]) + (mul(left[0], right[1]) + mul(left[1], right[0]))


def grids(shape):
    return lax.broadcasted_iota(jnp.int32, shape, 0), lax.broadcasted_iota(jnp.int32, shape, 1)


def unit_lower(values, first_row):
    rows, cols = grids(values.shape)
    rows = rows + first_row
    return jnp.where(rows > cols, values, jnp.where(rows == cols, F32(1.0), F32(0.0)))


def triangle_factor(values):
    rows, cols = grids(values.shape)
    scale = 2.0 / math.sqrt(values.shape[-1])
    return jnp.where(rows == cols, values, jnp.where(cols > rows, (values - 1.0) * scale, F32(0.0)))


def upper_part(values):
    rows, cols = grids(values.shape)
    return jnp.where(cols >= rows, values, F32(0.0))


def mix_level(leads, tree_v, tree_t, high, low):
    width = tree_v.shape[0]
    vees = upper_part(tree_v)
    tees = split(triangle_factor(tree_t).T)

    @pl.when(leads)
    def _():
        high[:, :width], low[:, :width] = tees
        high[:, width:], low[:, width:] = split(dot3(tees, split(vees.T)))

    @pl.when(jnp.logical_not(leads))
    def _():
        both = split(dot3(split(vees), tees))
        high[:, width:], low[:, width:] = both
        high[:, :width], low[:, :width] = split(dot3(both, split(vees.T)))


def start_all(pairs, sems):
    copies = [pltpu.make_async_copy(a, b, sems.at[i]) for i, (a, b) in enumerate(pairs)]
    for copy in copies:
        copy.start()
    return copies


def prepare_kernel(place, panel_t, tree_v, tree_t, trailing, th, tl, *args):
    mixes, (block, tri, vee, tee, sems) = args[:-5], args[-5:]
    ahead = len(mixes) // 2
    pairs = [(panel_t, tri)]
    for level in range(ahead):
        pairs += [(tree_v.at[level], vee.at[level]), (tree_t.at[level], tee.at[level])]
    copies = start_all(pairs + [(trailing, block)], sems)
    copies[0].wait()
    th[...], tl[...] = split(triangle_factor(tri[...]).T)
    for level in range(ahead):
        copies[2 * level + 1].wait()
        copies[2 * level + 2].wait()
        mix_level((place[0] >> level) & 1 == 0, vee[level], tee[level], *mixes[2 * level : 2 * level + 2])
    copies[-1].wait()


def mixes_kernel(level, place, tree_v, tree_t, after, high, low, vee, tee, sems):
    del after
    for copy in start_all(((tree_v.at[level], vee), (tree_t.at[level], tee)), sems):
        copy.wait()
    mix_level((place[0] >> level) & 1 == 0, vee[...], tee[...], high, low)


def opposite_rows(col, size, count):
    return pl.multiple_of(lax.rem(col + count // 2, count) * size, size)


def both_ways(rows, start):
    rows = unit_lower(rows, start)
    return split(rows), split(rows.T)


def early_kernel(place, own, left_a, left_b, right_a, right_b, block, partial, yh, yl, fh, fl):
    col = place[1]
    size = own.shape[0]
    count = block.shape[0] // size
    width = partial.shape[1]
    total = None
    for shift, parts in ((0, (own,)), (count - 1, (left_a, left_b)), (1, (right_a, right_b))):
        start = pl.multiple_of(lax.rem(col + shift, count) * size, size)
        rows = parts[0][...] if len(parts) == 1 else jnp.concatenate([p[...] for p in parts], axis=0)
        here = pl.ds(start, size)
        straight, flipped = both_ways(rows, start)
        yh[here, :], yl[here, :] = straight
        fh[:, here], fl[:, here] = flipped
        term = dot3(flipped, split(block[pl.ds(start, size), :width]))
        total = term if total is None else total + term
    partial[...] = total


def store_parts(value, parts):
    first = 0
    for part in parts:
        part[...] = value[:, first : first + part.shape[1]]
        first += part.shape[1]


def first_kernel(place, partial, opp_a, opp_b, block, th, tl, yh, yl, top, proj, gh, gl, oh, ol, ph, plow):
    size = 2 * opp_a.shape[0]
    width = partial.shape[1]
    start = opposite_rows(place[1], size, block.shape[0] // size)
    rows = jnp.concatenate([opp_a[...], opp_b[...]], axis=0)
    straight, flipped = both_ways(rows, start)
    upper = [jnp.where(start == 0, new, old[:size, :]) for new, old in zip(straight, (yh, yl))]
    gain = split(dot3(upper, (th[...], tl[...])))
    value = partial[...] + dot3(flipped, split(block[pl.ds(start, size), :width]))
    top[...] = block[:size, :width] - dot3(gain, split(value))
    proj[...] = value
    gh[...], gl[...] = gain
    oh[...], ol[...] = straight
    ph[...], plow[...] = flipped


def assemble_kernel(place, yh_in, yl_in, fh_in, fl_in, oh, ol, ph, plow, yh, yl, fh, fl):
    size = oh.shape[0]
    here = pl.ds(opposite_rows(place[1], size, yh.shape[0] // size), size)
    for out, old, new in ((yh, yh_in, oh), (yl, yl_in, ol)):
        out[...] = old[...]
        out[here, :] = new[...]
    for out, old, new in ((fh, fh_in, ph), (fl, fl_in, plow)):
        out[...] = old[...]
        out[:, here] = new[...]


def next_kernel(span, block, fh, fl, gh, gl, top, proj):
    values = block[:, span]
    value = dot3((fh[...], fl[...]), split(values))
    top[...] = values[: top.shape[0]] - dot3((gh[...], gl[...]), split(value))
    proj[...] = value


def rest_kernel(first, block, yh, yl, th, tl, *args):
    projs, (out, slots, sems) = args[: -3 - (first > 0)], args[-3:]
    count, size, width = slots.shape
    weights = [split(dot3((th[...], tl[...]), split(proj[...]))) for proj in projs]
    copies = []
    for i in range(count):
        here = slice((i + 1) * size, (i + 2) * size)
        at = 0
        for weight in weights:
            wide = weight[0].shape[1]
            values = block[here, first + at : first + at + wide]
            slots[i, :, at : at + wide] = values - dot3((yh[here, :], yl[here, :]), weight)
            at += wide
        target = out.at[pl.ds((i + 1) * size, size), pl.ds(first, width)]
        copies.append(pltpu.make_async_copy(slots.at[i], target, sems.at[i]))
        copies[-1].start()
    for copy in copies:
        copy.wait()


def mixed(mine, theirs, high, low):
    width = mine.shape[0]
    one = dot3((high[:, :width], low[:, :width]), split(mine[...]))
    two = dot3((high[:, width:], low[:, width:]), split(theirs[...]))
    return mine[...] - (one + two)


def level_kernel(mine, theirs, high, low, *parts):
    store_parts(mixed(mine, theirs, high, low), parts)


def final_kernel(first, mine, theirs, high, low, whole, out, slot, sem):
    del whole
    slot[...] = mixed(mine, theirs, high, low)
    copy = pltpu.make_async_copy(slot, out.at[pl.ds(0, slot.shape[0]), pl.ds(first, slot.shape[1])], sem)
    copy.start()
    copy.wait()


def shaped(shape, dtype=F32):
    return jax.ShapeDtypeStruct(shape, dtype)


def layout():
    units, chunks, first = [], [], 0
    for unit in UNITS:
        units.append((first, sum(unit)))
        for w in unit:
            chunks.append((first, w))
            first += w
    return units, chunks


def call(kernel, **options):
    mib = options.pop("mib")
    flops, moved = options.pop("cost")
    return pl.pallas_call(
        kernel,
        compiler_params=pltpu.CompilerParams(vmem_limit_bytes=mib << 20),
        cost_estimate=pl.CostEstimate(flops=flops, bytes_accessed=moved, transcendentals=0),
        **options,
    )


def fixed(values):
    return pltpu.with_memory_space_constraint(values, pltpu.HBM)


def update(trailing, panel_y, panel_t, tree_v, tree_t):
    size, width = panel_y.shape
    rows, columns = trailing.shape
    levels = tree_v.shape[0]
    half = size // 2
    count = lax.axis_size("col")
    place = jnp.stack([lax.axis_index("row"), lax.axis_index("col")]).astype(jnp.int32)
    onward = [(c, (c + 1) % count) for c in range(count)]
    backward = [(c, (c - 1) % count) for c in range(count)]

    own_a, own_b = panel_y[:half], panel_y[half:]
    left_a = lax.ppermute(own_a, "col", onward)
    right_b = lax.ppermute(own_b, "col", backward)
    left_b = lax.ppermute(own_b, "col", onward)
    right_a = lax.ppermute(own_a, "col", backward)
    opp_a = lax.ppermute(left_a, "col", onward)
    opp_b = lax.ppermute(right_b, "col", backward)

    square = shaped((width, width), BF16)
    mix = shaped((width, 2 * width), BF16)
    tall = shaped((rows, width), BF16)
    wide = shaped((width, rows), BF16)
    cube = 2 * 3 * width**3
    trailing = fixed(trailing)
    panel_t, tree_v, tree_t = fixed(panel_t), fixed(tree_v), fixed(tree_t)
    units, chunks = layout()
    ahead = levels - 1
    th, tl, *mixes, block = call(
        prepare_kernel,
        out_shape=[square, square] + [mix] * (2 * ahead) + [shaped((rows, columns))],
        in_specs=[SMEM] + [HBM] * 4,
        out_specs=[VMEM] * (3 + 2 * ahead),
        scratch_shapes=[pltpu.VMEM((width, width), F32)]
        + [pltpu.VMEM((ahead, width, width), F32)] * 2
        + [pltpu.SemaphoreType.DMA((2 * ahead + 2,))],
        mib=16,
        cost=(5 * cube, 5 << 20),
    )(place, panel_t, tree_v, tree_t, trailing)

    w = units[0][1]
    partial, yh, yl, fh, fl = call(
        early_kernel,
        out_shape=[shaped((width, w)), tall, tall, wide, wide],
        in_specs=[SMEM] + [VMEM] * 6,
        out_specs=[VMEM] * 5,
        mib=16,
        cost=(2 * cube, 4 << 20),
    )(place, panel_y, left_a, left_b, right_a, right_b, block)

    top, proj, gh, gl, *opposite = call(
        first_kernel,
        out_shape=[shaped((width, w))] * 2 + [square] * 6,
        in_specs=[SMEM] + [VMEM] * 8,
        out_specs=[VMEM] * 8,
        mib=16,
        cost=(2 * cube, 2 << 20),
    )(place, partial, opp_a, opp_b, block, th, tl, yh, yl)

    yh, yl, fh, fl = call(
        assemble_kernel,
        out_shape=[tall, tall, wide, wide],
        in_specs=[SMEM] + [VMEM] * 8,
        out_specs=[VMEM] * 4,
        mib=16,
        cost=(0, 4 << 20),
    )(place, yh, yl, fh, fl, *opposite)

    def swap(level, values):
        route = [(r, r ^ (1 << level)) for r in range(lax.axis_size("row"))]
        return lax.ppermute(values, "row", route)

    def combine(level, values, widths):
        w = values.shape[1]
        return call(
            level_kernel,
            out_shape=[shaped((width, w)) for w in widths],
            in_specs=[VMEM] * 4,
            out_specs=[VMEM] * len(widths),
            mib=8,
            cost=(2 * cube * w // width, 1 << 20),
        )(values, swap(level, values), *mixes[2 * level : 2 * level + 2])

    tops, projs = [], []
    for u, (first, w) in enumerate(units):
        if u:
            top, proj = call(
                functools.partial(next_kernel, slice(first, first + w)),
                out_shape=[shaped((width, w))] * 2,
                in_specs=[VMEM] * 5,
                out_specs=[VMEM] * 2,
                mib=16,
                cost=(5 * cube * w // width, 2 << 20),
            )(block, fh, fl, gh, gl)
        projs.append(proj)
        tops += combine(0, top, UNITS[u])

    for level in range(1, levels - 1):
        tops = [combine(level, top, (top.shape[1],))[0] for top in tops]

    level = levels - 1
    mixes += call(
        functools.partial(mixes_kernel, level),
        out_shape=[mix] * 2,
        in_specs=[SMEM] + [HBM] * 2 + [ANY],
        out_specs=[VMEM] * 2,
        scratch_shapes=[pltpu.VMEM((width, width), F32)] * 2 + [pltpu.SemaphoreType.DMA((2,))],
        mib=8,
        cost=(2 * cube, 1 << 20),
    )(place, tree_v, tree_t, projs[-1])

    out = ()
    parts = rows // size - 1
    for group in ((0, 1), (2, 3)):
        first = units[group[0]][0]
        w = sum(units[u][1] for u in group)
        out = (
            call(
                functools.partial(rest_kernel, first),
                out_shape=shaped((rows, columns)),
                in_specs=[VMEM] * (5 + len(group)) + [HBM] * len(out),
                out_specs=HBM,
                scratch_shapes=[pltpu.VMEM((parts, size, w), F32), pltpu.SemaphoreType.DMA((parts,))],
                input_output_aliases={5 + len(group): 0} if out else {},
                mib=16,
                cost=(10 * cube, 4 << 20),
            )(block, yh, yl, th, tl, *[projs[u] for u in group], *out),
        )
    out = out[0]

    for k, (first, w) in enumerate(chunks):
        out = call(
            functools.partial(final_kernel, first),
            out_shape=shaped((rows, columns)),
            in_specs=[VMEM] * 4 + [HBM],
            out_specs=HBM,
            scratch_shapes=[pltpu.VMEM((width, w), F32), pltpu.SemaphoreType.DMA],
            input_output_aliases={4: 0},
            mib=8,
            cost=(2 * cube * w // width, 1 << 20),
        )(tops[k], swap(level, tops[k]), *mixes[2 * level :], out)
    return out


def solution(mesh):
    placed = (
        P("row", "col"),
        P(("row", "col"), None),
        P("row", None),
        P(None, "row", None),
        P(None, "row", None),
    )
    return jax.shard_map(
        update, mesh=mesh, in_specs=placed, out_specs=P("row", "col"), check_vma=False
    )
```

```python
import functools
import math

import jax
import jax.numpy as jnp
from jax import lax
from jax.experimental import pallas as pl
from jax.experimental.pallas import tpu as pltpu
from jax.sharding import PartitionSpec as P


UNITS = ((128, 128), (128, 128), (256,), (256,))
F32 = jnp.float32
BF16 = jnp.bfloat16
VMEM = pl.BlockSpec(memory_space=pltpu.VMEM)
SMEM = pl.BlockSpec(memory_space=pltpu.SMEM)
HBM = pl.BlockSpec(memory_space=pltpu.HBM)
ANY = pl.BlockSpec(memory_space=pl.ANY)


def split(values):
    high = values.astype(BF16)
    return high, (values - high.astype(F32)).astype(BF16)


def dot3(left, right):
    mul = functools.partial(jnp.dot, preferred_element_type=F32)
    return mul(left[0], right[0]) + (mul(left[0], right[1]) + mul(left[1], right[0]))


def grids(shape):
    return lax.broadcasted_iota(jnp.int32, shape, 0), lax.broadcasted_iota(jnp.int32, shape, 1)


def unit_lower(values, first_row):
    rows, cols = grids(values.shape)
    rows = rows + first_row
    return jnp.where(rows > cols, values, jnp.where(rows == cols, F32(1.0), F32(0.0)))


def triangle_factor(values):
    rows, cols = grids(values.shape)
    scale = 2.0 / math.sqrt(values.shape[-1])
    return jnp.where(rows == cols, values, jnp.where(cols > rows, (values - 1.0) * scale, F32(0.0)))


def upper_part(values):
    rows, cols = grids(values.shape)
    return jnp.where(cols >= rows, values, F32(0.0))


def mix_level(leads, tree_v, tree_t, high, low):
    width = tree_v.shape[0]
    vees = upper_part(tree_v)
    tees = split(triangle_factor(tree_t).T)

    @pl.when(leads)
    def _():
        high[:, :width], low[:, :width] = tees
        high[:, width:], low[:, width:] = split(dot3(tees, split(vees.T)))

    @pl.when(jnp.logical_not(leads))
    def _():
        both = split(dot3(split(vees), tees))
        high[:, width:], low[:, width:] = both
        high[:, :width], low[:, :width] = split(dot3(both, split(vees.T)))


def start_all(pairs, sems):
    copies = [pltpu.make_async_copy(a, b, sems.at[i]) for i, (a, b) in enumerate(pairs)]
    for copy in copies:
        copy.start()
    return copies


def prepare_kernel(place, panel_t, tree_v, tree_t, trailing, th, tl, *args):
    mixes, (block, tri, vee, tee, sems) = args[:-5], args[-5:]
    ahead = len(mixes) // 2
    pairs = [(panel_t, tri)]
    for level in range(ahead):
        pairs += [(tree_v.at[level], vee.at[level]), (tree_t.at[level], tee.at[level])]
    copies = start_all(pairs + [(trailing, block)], sems)
    copies[0].wait()
    th[...], tl[...] = split(triangle_factor(tri[...]).T)
    for level in range(ahead):
        copies[2 * level + 1].wait()
        copies[2 * level + 2].wait()
        mix_level((place[0] >> level) & 1 == 0, vee[level], tee[level], *mixes[2 * level : 2 * level + 2])
    copies[-1].wait()


def mixes_kernel(level, place, tree_v, tree_t, after, high, low, vee, tee, sems):
    del after
    for copy in start_all(((tree_v.at[level], vee), (tree_t.at[level], tee)), sems):
        copy.wait()
    mix_level((place[0] >> level) & 1 == 0, vee[...], tee[...], high, low)


def opposite_rows(col, size, count):
    return pl.multiple_of(lax.rem(col + count // 2, count) * size, size)


def both_ways(rows, start):
    rows = unit_lower(rows, start)
    return split(rows), split(rows.T)


def early_kernel(place, own, left, right_a, right_b, block, partial, yh, yl, fh, fl):
    col = place[1]
    size = own.shape[0]
    count = block.shape[0] // size
    width = partial.shape[1]
    total = None
    for shift, parts in ((0, (own,)), (count - 1, (left,)), (1, (right_a, right_b))):
        start = pl.multiple_of(lax.rem(col + shift, count) * size, size)
        rows = parts[0][...] if len(parts) == 1 else jnp.concatenate([p[...] for p in parts], axis=0)
        here = pl.ds(start, size)
        straight, flipped = both_ways(rows, start)
        yh[here, :], yl[here, :] = straight
        fh[:, here], fl[:, here] = flipped
        term = dot3(flipped, split(block[pl.ds(start, size), :width]))
        total = term if total is None else total + term
    partial[...] = total


def store_parts(value, parts):
    first = 0
    for part in parts:
        part[...] = value[:, first : first + part.shape[1]]
        first += part.shape[1]


def first_kernel(place, partial, opp_a, opp_b, block, th, tl, yh, yl, top, proj, gh, gl, oh, ol, ph, plow):
    size = opp_a.shape[0] + opp_b.shape[0]
    width = partial.shape[1]
    start = opposite_rows(place[1], size, block.shape[0] // size)
    rows = jnp.concatenate([opp_a[...], opp_b[...]], axis=0)
    straight, flipped = both_ways(rows, start)
    upper = [jnp.where(start == 0, new, old[:size, :]) for new, old in zip(straight, (yh, yl))]
    gain = split(dot3(upper, (th[...], tl[...])))
    value = partial[...] + dot3(flipped, split(block[pl.ds(start, size), :width]))
    top[...] = block[:size, :width] - dot3(gain, split(value))
    proj[...] = value
    gh[...], gl[...] = gain
    oh[...], ol[...] = straight
    ph[...], plow[...] = flipped


def assemble_kernel(place, yh_in, yl_in, fh_in, fl_in, oh, ol, ph, plow, yh, yl, fh, fl):
    size = oh.shape[0]
    here = pl.ds(opposite_rows(place[1], size, yh.shape[0] // size), size)
    for out, old, new in ((yh, yh_in, oh), (yl, yl_in, ol)):
        out[...] = old[...]
        out[here, :] = new[...]
    for out, old, new in ((fh, fh_in, ph), (fl, fl_in, plow)):
        out[...] = old[...]
        out[:, here] = new[...]


def next_kernel(span, block, fh, fl, gh, gl, top, proj):
    values = block[:, span]
    value = dot3((fh[...], fl[...]), split(values))
    top[...] = values[: top.shape[0]] - dot3((gh[...], gl[...]), split(value))
    proj[...] = value


def rest_kernel(first, block, yh, yl, th, tl, *args):
    projs, (out, slots, sems) = args[: -3 - (first > 0)], args[-3:]
    count, size, width = slots.shape
    weights = [split(dot3((th[...], tl[...]), split(proj[...]))) for proj in projs]
    copies = []
    for i in range(count):
        here = slice((i + 1) * size, (i + 2) * size)
        at = 0
        for weight in weights:
            wide = weight[0].shape[1]
            values = block[here, first + at : first + at + wide]
            slots[i, :, at : at + wide] = values - dot3((yh[here, :], yl[here, :]), weight)
            at += wide
        target = out.at[pl.ds((i + 1) * size, size), pl.ds(first, width)]
        copies.append(pltpu.make_async_copy(slots.at[i], target, sems.at[i]))
        copies[-1].start()
    for copy in copies:
        copy.wait()


def mixed(mine, theirs, high, low):
    width = mine.shape[0]
    one = dot3((high[:, :width], low[:, :width]), split(mine[...]))
    two = dot3((high[:, width:], low[:, width:]), split(theirs[...]))
    return mine[...] - (one + two)


def level_kernel(mine, theirs, high, low, *parts):
    store_parts(mixed(mine, theirs, high, low), parts)


def final_kernel(first, mine, theirs, high, low, whole, out, slot, sem):
    del whole
    slot[...] = mixed(mine, theirs, high, low)
    copy = pltpu.make_async_copy(slot, out.at[pl.ds(0, slot.shape[0]), pl.ds(first, slot.shape[1])], sem)
    copy.start()
    copy.wait()


def shaped(shape, dtype=F32):
    return jax.ShapeDtypeStruct(shape, dtype)


def layout():
    units, chunks, first = [], [], 0
    for unit in UNITS:
        units.append((first, sum(unit)))
        for w in unit:
            chunks.append((first, w))
            first += w
    return units, chunks


def call(kernel, **options):
    mib = options.pop("mib")
    flops, moved = options.pop("cost")
    return pl.pallas_call(
        kernel,
        compiler_params=pltpu.CompilerParams(vmem_limit_bytes=mib << 20),
        cost_estimate=pl.CostEstimate(flops=flops, bytes_accessed=moved, transcendentals=0),
        **options,
    )


def fixed(values):
    return pltpu.with_memory_space_constraint(values, pltpu.HBM)


def update(trailing, panel_y, panel_t, tree_v, tree_t):
    size, width = panel_y.shape
    rows, columns = trailing.shape
    levels = tree_v.shape[0]
    cut = size * 7 // 16
    count = lax.axis_size("col")
    place = jnp.stack([lax.axis_index("row"), lax.axis_index("col")]).astype(jnp.int32)
    onward = [(c, (c + 1) % count) for c in range(count)]
    backward = [(c, (c - 1) % count) for c in range(count)]

    left = lax.ppermute(panel_y, "col", onward)
    right_b = lax.ppermute(panel_y[cut:], "col", backward)
    right_a = lax.ppermute(panel_y[:cut], "col", backward)
    opp_b = lax.ppermute(right_b, "col", backward)
    opp_a = lax.ppermute(left[:cut], "col", onward)

    square = shaped((width, width), BF16)
    mix = shaped((width, 2 * width), BF16)
    tall = shaped((rows, width), BF16)
    wide = shaped((width, rows), BF16)
    cube = 2 * 3 * width**3
    trailing = fixed(trailing)
    panel_t, tree_v, tree_t = fixed(panel_t), fixed(tree_v), fixed(tree_t)
    units, chunks = layout()
    ahead = levels - 1
    th, tl, *mixes, block = call(
        prepare_kernel,
        out_shape=[square, square] + [mix] * (2 * ahead) + [shaped((rows, columns))],
        in_specs=[SMEM] + [HBM] * 4,
        out_specs=[VMEM] * (3 + 2 * ahead),
        scratch_shapes=[pltpu.VMEM((width, width), F32)]
        + [pltpu.VMEM((ahead, width, width), F32)] * 2
        + [pltpu.SemaphoreType.DMA((2 * ahead + 2,))],
        mib=16,
        cost=(5 * cube, 5 << 20),
    )(place, panel_t, tree_v, tree_t, trailing)

    w = units[0][1]
    partial, yh, yl, fh, fl = call(
        early_kernel,
        out_shape=[shaped((width, w)), tall, tall, wide, wide],
        in_specs=[SMEM] + [VMEM] * 5,
        out_specs=[VMEM] * 5,
        mib=16,
        cost=(2 * cube, 4 << 20),
    )(place, panel_y, left, right_a, right_b, block)

    top, proj, gh, gl, *opposite = call(
        first_kernel,
        out_shape=[shaped((width, w))] * 2 + [square] * 6,
        in_specs=[SMEM] + [VMEM] * 8,
        out_specs=[VMEM] * 8,
        mib=16,
        cost=(2 * cube, 2 << 20),
    )(place, partial, opp_a, opp_b, block, th, tl, yh, yl)

    yh, yl, fh, fl = call(
        assemble_kernel,
        out_shape=[tall, tall, wide, wide],
        in_specs=[SMEM] + [VMEM] * 8,
        out_specs=[VMEM] * 4,
        mib=16,
        cost=(0, 4 << 20),
    )(place, yh, yl, fh, fl, *opposite)

    def swap(level, values):
        route = [(r, r ^ (1 << level)) for r in range(lax.axis_size("row"))]
        return lax.ppermute(values, "row", route)

    def combine(level, values, widths):
        w = values.shape[1]
        return call(
            level_kernel,
            out_shape=[shaped((width, w)) for w in widths],
            in_specs=[VMEM] * 4,
            out_specs=[VMEM] * len(widths),
            mib=8,
            cost=(2 * cube * w // width, 1 << 20),
        )(values, swap(level, values), *mixes[2 * level : 2 * level + 2])

    tops, projs = [], []
    for u, (first, w) in enumerate(units):
        if u:
            top, proj = call(
                functools.partial(next_kernel, slice(first, first + w)),
                out_shape=[shaped((width, w))] * 2,
                in_specs=[VMEM] * 5,
                out_specs=[VMEM] * 2,
                mib=16,
                cost=(5 * cube * w // width, 2 << 20),
            )(block, fh, fl, gh, gl)
        projs.append(proj)
        tops += combine(0, top, UNITS[u])

    for level in range(1, levels - 1):
        tops = [combine(level, top, (top.shape[1],))[0] for top in tops]

    level = levels - 1
    mixes += call(
        functools.partial(mixes_kernel, level),
        out_shape=[mix] * 2,
        in_specs=[SMEM] + [HBM] * 2 + [ANY],
        out_specs=[VMEM] * 2,
        scratch_shapes=[pltpu.VMEM((width, width), F32)] * 2 + [pltpu.SemaphoreType.DMA((2,))],
        mib=8,
        cost=(2 * cube, 1 << 20),
    )(place, tree_v, tree_t, projs[-1])

    out = ()
    parts = rows // size - 1
    for group in ((0, 1), (2, 3)):
        first = units[group[0]][0]
        w = sum(units[u][1] for u in group)
        out = (
            call(
                functools.partial(rest_kernel, first),
                out_shape=shaped((rows, columns)),
                in_specs=[VMEM] * (5 + len(group)) + [HBM] * len(out),
                out_specs=HBM,
                scratch_shapes=[pltpu.VMEM((parts, size, w), F32), pltpu.SemaphoreType.DMA((parts,))],
                input_output_aliases={5 + len(group): 0} if out else {},
                mib=16,
                cost=(10 * cube, 4 << 20),
            )(block, yh, yl, th, tl, *[projs[u] for u in group], *out),
        )
    out = out[0]

    for k, (first, w) in enumerate(chunks):
        out = call(
            functools.partial(final_kernel, first),
            out_shape=shaped((rows, columns)),
            in_specs=[VMEM] * 4 + [HBM],
            out_specs=HBM,
            scratch_shapes=[pltpu.VMEM((width, w), F32), pltpu.SemaphoreType.DMA],
            input_output_aliases={4: 0},
            mib=8,
            cost=(2 * cube * w // width, 1 << 20),
        )(tops[k], swap(level, tops[k]), *mixes[2 * level :], out)
    return out


def solution(mesh):
    placed = (
        P("row", "col"),
        P(("row", "col"), None),
        P("row", None),
        P(None, "row", None),
        P(None, "row", None),
    )
    return jax.shard_map(
        update, mesh=mesh, in_specs=placed, out_specs=P("row", "col"), check_vma=False
    )
```

```python
import functools
import math

import jax
import jax.numpy as jnp
from jax import lax
from jax.experimental import pallas as pl
from jax.experimental.pallas import tpu as pltpu
from jax.sharding import PartitionSpec as P


UNITS = ((128, 128), (128, 128), (256,), (256,))
F32 = jnp.float32
BF16 = jnp.bfloat16
VMEM = pl.BlockSpec(memory_space=pltpu.VMEM)
SMEM = pl.BlockSpec(memory_space=pltpu.SMEM)
HBM = pl.BlockSpec(memory_space=pltpu.HBM)
ANY = pl.BlockSpec(memory_space=pl.ANY)


def split(values):
    high = values.astype(BF16)
    return high, (values - high.astype(F32)).astype(BF16)


def dot3(left, right):
    mul = functools.partial(jnp.dot, preferred_element_type=F32)
    return mul(left[0], right[0]) + (mul(left[0], right[1]) + mul(left[1], right[0]))


def grids(shape):
    return lax.broadcasted_iota(jnp.int32, shape, 0), lax.broadcasted_iota(jnp.int32, shape, 1)


def unit_lower(values, first_row):
    rows, cols = grids(values.shape)
    rows = rows + first_row
    return jnp.where(rows > cols, values, jnp.where(rows == cols, F32(1.0), F32(0.0)))


def triangle_factor(values):
    rows, cols = grids(values.shape)
    scale = 2.0 / math.sqrt(values.shape[-1])
    return jnp.where(rows == cols, values, jnp.where(cols > rows, (values - 1.0) * scale, F32(0.0)))


def upper_part(values):
    rows, cols = grids(values.shape)
    return jnp.where(cols >= rows, values, F32(0.0))


def mix_level(leads, tree_v, tree_t, high, low):
    width = tree_v.shape[0]
    vees = upper_part(tree_v)
    tees = split(triangle_factor(tree_t).T)

    @pl.when(leads)
    def _():
        high[:, :width], low[:, :width] = tees
        high[:, width:], low[:, width:] = split(dot3(tees, split(vees.T)))

    @pl.when(jnp.logical_not(leads))
    def _():
        both = split(dot3(split(vees), tees))
        high[:, width:], low[:, width:] = both
        high[:, :width], low[:, :width] = split(dot3(both, split(vees.T)))


def start_all(pairs, sems):
    copies = [pltpu.make_async_copy(a, b, sems.at[i]) for i, (a, b) in enumerate(pairs)]
    for copy in copies:
        copy.start()
    return copies


def halves_kernel(panel, first, second, sems):
    cut = first.shape[0]
    for copy in start_all(((panel.at[:cut], first), (panel.at[cut:], second)), sems):
        copy.wait()


def prepare_kernel(place, panel_t, tree_v, tree_t, trailing, th, tl, *args):
    mixes, (block, tri, vee, tee, sems) = args[:-5], args[-5:]
    ahead = len(mixes) // 2
    pairs = [(panel_t, tri)]
    for level in range(ahead):
        pairs += [(tree_v.at[level], vee.at[level]), (tree_t.at[level], tee.at[level])]
    copies = start_all(pairs + [(trailing.at[:, : block.shape[1]], block)], sems)
    copies[0].wait()
    th[...], tl[...] = split(triangle_factor(tri[...]).T)
    for level in range(ahead):
        copies[2 * level + 1].wait()
        copies[2 * level + 2].wait()
        mix_level((place[0] >> level) & 1 == 0, vee[level], tee[level], *mixes[2 * level : 2 * level + 2])
    copies[-1].wait()


def mixes_kernel(level, place, tree_v, tree_t, after, high, low, vee, tee, sems):
    del after
    for copy in start_all(((tree_v.at[level], vee), (tree_t.at[level], tee)), sems):
        copy.wait()
    mix_level((place[0] >> level) & 1 == 0, vee[...], tee[...], high, low)


def opposite_rows(col, size, count):
    return pl.multiple_of(lax.rem(col + count // 2, count) * size, size)


def both_ways(rows, start):
    rows = unit_lower(rows, start)
    return split(rows), split(rows.T)


def early_kernel(place, own_a, own_b, left_a, left_b, right_a, right_b, block, partial, yh, yl, fh, fl):
    col = place[1]
    size = own_a.shape[0] + own_b.shape[0]
    count = block.shape[0] // size
    width = partial.shape[1]
    total = None
    for shift, parts in ((0, (own_a, own_b)), (count - 1, (left_a, left_b)), (1, (right_a, right_b))):
        start = pl.multiple_of(lax.rem(col + shift, count) * size, size)
        rows = jnp.concatenate([p[...] for p in parts], axis=0)
        here = pl.ds(start, size)
        straight, flipped = both_ways(rows, start)
        yh[here, :], yl[here, :] = straight
        fh[:, here], fl[:, here] = flipped
        term = dot3(flipped, split(block[pl.ds(start, size), :width]))
        total = term if total is None else total + term
    partial[...] = total


def store_parts(value, parts):
    first = 0
    for part in parts:
        part[...] = value[:, first : first + part.shape[1]]
        first += part.shape[1]


def first_kernel(place, partial, opp_a, opp_b, block, th, tl, yh, yl, top, proj, gh, gl, oh, ol, ph, plow):
    size = opp_a.shape[0] + opp_b.shape[0]
    width = partial.shape[1]
    start = opposite_rows(place[1], size, block.shape[0] // size)
    rows = jnp.concatenate([opp_a[...], opp_b[...]], axis=0)
    straight, flipped = both_ways(rows, start)
    upper = [jnp.where(start == 0, new, old[:size, :]) for new, old in zip(straight, (yh, yl))]
    gain = split(dot3(upper, (th[...], tl[...])))
    value = partial[...] + dot3(flipped, split(block[pl.ds(start, size), :width]))
    top[...] = block[:size, :width] - dot3(gain, split(value))
    proj[...] = value
    gh[...], gl[...] = gain
    oh[...], ol[...] = straight
    ph[...], plow[...] = flipped


def assemble_kernel(place, yh_in, yl_in, fh_in, fl_in, oh, ol, ph, plow, yh, yl, fh, fl):
    size = oh.shape[0]
    here = pl.ds(opposite_rows(place[1], size, yh.shape[0] // size), size)
    for out, old, new in ((yh, yh_in, oh), (yl, yl_in, ol)):
        out[...] = old[...]
        out[here, :] = new[...]
    for out, old, new in ((fh, fh_in, ph), (fl, fl_in, plow)):
        out[...] = old[...]
        out[:, here] = new[...]


def next_kernel(span, block, fh, fl, gh, gl, top, proj):
    values = block[:, span]
    value = dot3((fh[...], fl[...]), split(values))
    top[...] = values[: top.shape[0]] - dot3((gh[...], gl[...]), split(value))
    proj[...] = value


def rest_kernel(first, block, yh, yl, th, tl, *args):
    projs, (out, slots, sems) = args[: -3 - (first > 0)], args[-3:]
    count, size, width = slots.shape
    weights = [split(dot3((th[...], tl[...]), split(proj[...]))) for proj in projs]
    copies = []
    for i in range(count):
        here = slice((i + 1) * size, (i + 2) * size)
        at = 0
        for weight in weights:
            wide = weight[0].shape[1]
            values = block[here, first + at : first + at + wide]
            slots[i, :, at : at + wide] = values - dot3((yh[here, :], yl[here, :]), weight)
            at += wide
        target = out.at[pl.ds((i + 1) * size, size), pl.ds(first, width)]
        copies.append(pltpu.make_async_copy(slots.at[i], target, sems.at[i]))
        copies[-1].start()
    for copy in copies:
        copy.wait()


def mixed(mine, theirs, high, low):
    width = mine.shape[0]
    one = dot3((high[:, :width], low[:, :width]), split(mine[...]))
    two = dot3((high[:, width:], low[:, width:]), split(theirs[...]))
    return mine[...] - (one + two)


def level_kernel(mine, theirs, high, low, *parts):
    store_parts(mixed(mine, theirs, high, low), parts)


def final_kernel(first, mine, theirs, high, low, whole, out, slot, sem):
    del whole
    slot[...] = mixed(mine, theirs, high, low)
    copy = pltpu.make_async_copy(slot, out.at[pl.ds(0, slot.shape[0]), pl.ds(first, slot.shape[1])], sem)
    copy.start()
    copy.wait()


def shaped(shape, dtype=F32):
    return jax.ShapeDtypeStruct(shape, dtype)


def layout():
    units, chunks, first = [], [], 0
    for unit in UNITS:
        units.append((first, sum(unit)))
        for w in unit:
            chunks.append((first, w))
            first += w
    return units, chunks


def call(kernel, **options):
    mib = options.pop("mib")
    flops, moved = options.pop("cost")
    return pl.pallas_call(
        kernel,
        compiler_params=pltpu.CompilerParams(vmem_limit_bytes=mib << 20),
        cost_estimate=pl.CostEstimate(flops=flops, bytes_accessed=moved, transcendentals=0),
        **options,
    )


def fixed(values):
    return pltpu.with_memory_space_constraint(values, pltpu.HBM)


def update(trailing, panel_y, panel_t, tree_v, tree_t):
    size, width = panel_y.shape
    rows, columns = trailing.shape
    levels = tree_v.shape[0]
    cut = size * 9 // 16
    count = lax.axis_size("col")
    place = jnp.stack([lax.axis_index("row"), lax.axis_index("col")]).astype(jnp.int32)
    onward = [(c, (c + 1) % count) for c in range(count)]
    backward = [(c, (c - 1) % count) for c in range(count)]

    own_a, own_b = call(
        halves_kernel,
        out_shape=[shaped((cut, width)), shaped((size - cut, width))],
        in_specs=[HBM],
        out_specs=[VMEM] * 2,
        scratch_shapes=[pltpu.SemaphoreType.DMA((2,))],
        mib=4,
        cost=(0, 1 << 19),
    )(fixed(panel_y))
    left_a = lax.ppermute(own_a, "col", onward)
    right_b = lax.ppermute(own_b, "col", backward)
    left_b = lax.ppermute(own_b, "col", onward)
    right_a = lax.ppermute(own_a, "col", backward)
    opp_a = lax.ppermute(left_a, "col", onward)
    opp_b = lax.ppermute(right_b, "col", backward)

    square = shaped((width, width), BF16)
    mix = shaped((width, 2 * width), BF16)
    tall = shaped((rows, width), BF16)
    wide = shaped((width, rows), BF16)
    cube = 2 * 3 * width**3
    panel_t, tree_v, tree_t = fixed(panel_t), fixed(tree_v), fixed(tree_t)
    units, chunks = layout()
    ahead = levels - 1
    th, tl, *mixes, block = call(
        prepare_kernel,
        out_shape=[square, square] + [mix] * (2 * ahead) + [shaped((rows, units[0][1]))],
        in_specs=[SMEM] + [HBM] * 4,
        out_specs=[VMEM] * (3 + 2 * ahead),
        scratch_shapes=[pltpu.VMEM((width, width), F32)]
        + [pltpu.VMEM((ahead, width, width), F32)] * 2
        + [pltpu.SemaphoreType.DMA((2 * ahead + 2,))],
        mib=16,
        cost=(5 * cube, 5 << 20),
    )(place, panel_t, tree_v, tree_t, fixed(trailing))

    w = units[0][1]
    partial, yh, yl, fh, fl = call(
        early_kernel,
        out_shape=[shaped((width, w)), tall, tall, wide, wide],
        in_specs=[SMEM] + [VMEM] * 7,
        out_specs=[VMEM] * 5,
        mib=16,
        cost=(2 * cube, 4 << 20),
    )(place, own_a, own_b, left_a, left_b, right_a, right_b, block)

    top, proj, gh, gl, *opposite = call(
        first_kernel,
        out_shape=[shaped((width, w))] * 2 + [square] * 6,
        in_specs=[SMEM] + [VMEM] * 8,
        out_specs=[VMEM] * 8,
        mib=16,
        cost=(2 * cube, 2 << 20),
    )(place, partial, opp_a, opp_b, block, th, tl, yh, yl)

    yh, yl, fh, fl = call(
        assemble_kernel,
        out_shape=[tall, tall, wide, wide],
        in_specs=[SMEM] + [VMEM] * 8,
        out_specs=[VMEM] * 4,
        mib=16,
        cost=(0, 4 << 20),
    )(place, yh, yl, fh, fl, *opposite)

    def swap(level, values):
        route = [(r, r ^ (1 << level)) for r in range(lax.axis_size("row"))]
        return lax.ppermute(values, "row", route)

    def combine(level, values, widths):
        w = values.shape[1]
        return call(
            level_kernel,
            out_shape=[shaped((width, w)) for w in widths],
            in_specs=[VMEM] * 4,
            out_specs=[VMEM] * len(widths),
            mib=8,
            cost=(2 * cube * w // width, 1 << 20),
        )(values, swap(level, values), *mixes[2 * level : 2 * level + 2])

    tops, projs = [], []
    for u, (first, w) in enumerate(units):
        if u:
            top, proj = call(
                functools.partial(next_kernel, slice(first, first + w)),
                out_shape=[shaped((width, w))] * 2,
                in_specs=[VMEM] * 5,
                out_specs=[VMEM] * 2,
                mib=16,
                cost=(5 * cube * w // width, 2 << 20),
            )(trailing, fh, fl, gh, gl)
        projs.append(proj)
        tops += combine(0, top, UNITS[u])

    for level in range(1, levels - 1):
        tops = [combine(level, top, (top.shape[1],))[0] for top in tops]

    level = levels - 1
    mixes += call(
        functools.partial(mixes_kernel, level),
        out_shape=[mix] * 2,
        in_specs=[SMEM] + [HBM] * 2 + [ANY],
        out_specs=[VMEM] * 2,
        scratch_shapes=[pltpu.VMEM((width, width), F32)] * 2 + [pltpu.SemaphoreType.DMA((2,))],
        mib=8,
        cost=(2 * cube, 1 << 20),
    )(place, tree_v, tree_t, projs[-1])

    out = ()
    parts = rows // size - 1
    for group in ((0, 1), (2, 3)):
        first = units[group[0]][0]
        w = sum(units[u][1] for u in group)
        out = (
            call(
                functools.partial(rest_kernel, first),
                out_shape=shaped((rows, columns)),
                in_specs=[VMEM] * (5 + len(group)) + [HBM] * len(out),
                out_specs=HBM,
                scratch_shapes=[pltpu.VMEM((parts, size, w), F32), pltpu.SemaphoreType.DMA((parts,))],
                input_output_aliases={5 + len(group): 0} if out else {},
                mib=16,
                cost=(10 * cube, 4 << 20),
            )(trailing, yh, yl, th, tl, *[projs[u] for u in group], *out),
        )
    out = out[0]

    for k, (first, w) in enumerate(chunks):
        out = call(
            functools.partial(final_kernel, first),
            out_shape=shaped((rows, columns)),
            in_specs=[VMEM] * 4 + [HBM],
            out_specs=HBM,
            scratch_shapes=[pltpu.VMEM((width, w), F32), pltpu.SemaphoreType.DMA],
            input_output_aliases={4: 0},
            mib=8,
            cost=(2 * cube * w // width, 1 << 20),
        )(tops[k], swap(level, tops[k]), *mixes[2 * level :], out)
    return out


def solution(mesh):
    placed = (
        P("row", "col"),
        P(("row", "col"), None),
        P("row", None),
        P(None, "row", None),
        P(None, "row", None),
    )
    return jax.shard_map(update, mesh=mesh, in_specs=placed, out_specs=P("row", "col"), check_vma=False)
```

```python
import functools
import math

import jax
import jax.numpy as jnp
from jax import lax
from jax.experimental import pallas as pl
from jax.experimental.pallas import tpu as pltpu
from jax.sharding import PartitionSpec as P


UNITS = ((128, 128), (128, 128), (256,), (256,))
F32 = jnp.float32
BF16 = jnp.bfloat16
VMEM = pl.BlockSpec(memory_space=pltpu.VMEM)
SMEM = pl.BlockSpec(memory_space=pltpu.SMEM)
HBM = pl.BlockSpec(memory_space=pltpu.HBM)
ANY = pl.BlockSpec(memory_space=pl.ANY)


def split(values):
    high = values.astype(BF16)
    return high, (values - high.astype(F32)).astype(BF16)


def dot3(left, right):
    (lh, ll), (rh, rl) = left, right
    long = jnp.concatenate([lh, lh, ll], axis=1), jnp.concatenate([rh, rl, rh], axis=0)
    return jnp.dot(*long, preferred_element_type=F32)


def grids(shape):
    return lax.broadcasted_iota(jnp.int32, shape, 0), lax.broadcasted_iota(jnp.int32, shape, 1)


def unit_lower(values, first_row):
    rows, cols = grids(values.shape)
    rows = rows + first_row
    return jnp.where(rows > cols, values, jnp.where(rows == cols, F32(1.0), F32(0.0)))


def triangle_factor(values):
    rows, cols = grids(values.shape)
    scale = 2.0 / math.sqrt(values.shape[-1])
    return jnp.where(rows == cols, values, jnp.where(cols > rows, (values - 1.0) * scale, F32(0.0)))


def upper_part(values):
    rows, cols = grids(values.shape)
    return jnp.where(cols >= rows, values, F32(0.0))


def mix_level(leads, tree_v, tree_t, high, low):
    width = tree_v.shape[0]
    vees = upper_part(tree_v)
    tees = split(triangle_factor(tree_t).T)

    @pl.when(leads)
    def _():
        high[:, :width], low[:, :width] = tees
        high[:, width:], low[:, width:] = split(dot3(tees, split(vees.T)))

    @pl.when(jnp.logical_not(leads))
    def _():
        both = split(dot3(split(vees), tees))
        high[:, width:], low[:, width:] = both
        high[:, :width], low[:, :width] = split(dot3(both, split(vees.T)))


def start_all(pairs, sems):
    copies = [pltpu.make_async_copy(a, b, sems.at[i]) for i, (a, b) in enumerate(pairs)]
    for copy in copies:
        copy.start()
    return copies


def halves_kernel(panel, first, second, sems):
    cut = first.shape[0]
    for copy in start_all(((panel.at[:cut], first), (panel.at[cut:], second)), sems):
        copy.wait()


def prepare_kernel(panel_t, trailing, th, tl, block, tri, sems):
    copies = start_all(((panel_t, tri), (trailing.at[:, : block.shape[1]], block)), sems)
    copies[0].wait()
    th[...], tl[...] = split(triangle_factor(tri[...]).T)
    copies[1].wait()


def mixes_kernel(level, place, tree_v, tree_t, after, high, low):
    del after
    mix_level((place[0] >> level) & 1 == 0, tree_v[level], tree_t[level], high, low)


def opposite_rows(col, size, count):
    return pl.multiple_of(lax.rem(col + count // 2, count) * size, size)


def both_ways(rows, start):
    rows = unit_lower(rows, start)
    return split(rows), split(rows.T)


def early_kernel(place, own_a, own_b, left_a, left_b, right_a, right_b, block, partial, yh, yl, fh, fl):
    col = place[1]
    size = own_a.shape[0] + own_b.shape[0]
    count = block.shape[0] // size
    width = partial.shape[1]
    total = None
    for shift, parts in ((0, (own_a, own_b)), (count - 1, (left_a, left_b)), (1, (right_a, right_b))):
        start = pl.multiple_of(lax.rem(col + shift, count) * size, size)
        rows = jnp.concatenate([p[...] for p in parts], axis=0)
        here = pl.ds(start, size)
        straight, flipped = both_ways(rows, start)
        yh[here, :], yl[here, :] = straight
        fh[:, here], fl[:, here] = flipped
        term = dot3(flipped, split(block[pl.ds(start, size), :width]))
        total = term if total is None else total + term
    partial[...] = total


def store_parts(value, parts):
    first = 0
    for part in parts:
        part[...] = value[:, first : first + part.shape[1]]
        first += part.shape[1]


def first_kernel(place, partial, opp_a, opp_b, block, th, tl, yh, yl, top, proj, gh, gl, oh, ol, ph, plow):
    size = opp_a.shape[0] + opp_b.shape[0]
    width = partial.shape[1]
    start = opposite_rows(place[1], size, block.shape[0] // size)
    rows = jnp.concatenate([opp_a[...], opp_b[...]], axis=0)
    straight, flipped = both_ways(rows, start)
    upper = [jnp.where(start == 0, new, old[:size, :]) for new, old in zip(straight, (yh, yl))]
    gain = split(dot3(upper, (th[...], tl[...])))
    value = partial[...] + dot3(flipped, split(block[pl.ds(start, size), :width]))
    top[...] = block[:size, :width] - dot3(gain, split(value))
    proj[...] = value
    gh[...], gl[...] = gain
    oh[...], ol[...] = straight
    ph[...], plow[...] = flipped


def assemble_kernel(place, yh_in, yl_in, fh_in, fl_in, oh, ol, ph, plow, yh, yl, fh, fl):
    size = oh.shape[0]
    here = pl.ds(opposite_rows(place[1], size, yh.shape[0] // size), size)
    for out, old, new in ((yh, yh_in, oh), (yl, yl_in, ol)):
        out[...] = old[...]
        out[here, :] = new[...]
    for out, old, new in ((fh, fh_in, ph), (fl, fl_in, plow)):
        out[...] = old[...]
        out[:, here] = new[...]


def next_kernel(span, block, fh, fl, gh, gl, top, proj):
    values = block[:, span]
    value = dot3((fh[...], fl[...]), split(values))
    top[...] = values[: top.shape[0]] - dot3((gh[...], gl[...]), split(value))
    proj[...] = value


def rest_kernel(first, block, yh, yl, th, tl, *args):
    projs, (out, slots, sems) = args[: -3 - (first > 0)], args[-3:]
    count, size, width = slots.shape
    weights = [split(dot3((th[...], tl[...]), split(proj[...]))) for proj in projs]
    copies = []
    for i in range(count):
        here = slice((i + 1) * size, (i + 2) * size)
        at = 0
        for weight in weights:
            wide = weight[0].shape[1]
            values = block[here, first + at : first + at + wide]
            slots[i, :, at : at + wide] = values - dot3((yh[here, :], yl[here, :]), weight)
            at += wide
        target = out.at[pl.ds((i + 1) * size, size), pl.ds(first, width)]
        copies.append(pltpu.make_async_copy(slots.at[i], target, sems.at[i]))
        copies[-1].start()
    for copy in copies:
        copy.wait()


def mixed(mine, theirs, high, low):
    width = mine.shape[0]
    one = dot3((high[:, :width], low[:, :width]), split(mine[...]))
    two = dot3((high[:, width:], low[:, width:]), split(theirs[...]))
    return mine[...] - (one + two)


def level_kernel(mine, theirs, high, low, *parts):
    store_parts(mixed(mine, theirs, high, low), parts)


def final_kernel(first, mine, theirs, high, low, whole, out, slot, sem):
    del whole
    slot[...] = mixed(mine, theirs, high, low)
    copy = pltpu.make_async_copy(slot, out.at[pl.ds(0, slot.shape[0]), pl.ds(first, slot.shape[1])], sem)
    copy.start()
    copy.wait()


def shaped(shape, dtype=F32):
    return jax.ShapeDtypeStruct(shape, dtype)


def layout():
    units, chunks, first = [], [], 0
    for unit in UNITS:
        units.append((first, sum(unit)))
        for w in unit:
            chunks.append((first, w))
            first += w
    return units, chunks


def call(kernel, **options):
    mib = options.pop("mib")
    flops, moved = options.pop("cost")
    return pl.pallas_call(
        kernel,
        compiler_params=pltpu.CompilerParams(vmem_limit_bytes=mib << 20),
        cost_estimate=pl.CostEstimate(flops=flops, bytes_accessed=moved, transcendentals=0),
        **options,
    )


def fixed(values):
    return pltpu.with_memory_space_constraint(values, pltpu.HBM)


def update(trailing, panel_y, panel_t, tree_v, tree_t):
    size, width = panel_y.shape
    rows, columns = trailing.shape
    levels = tree_v.shape[0]
    cut = size * 9 // 16
    count = lax.axis_size("col")
    place = jnp.stack([lax.axis_index("row"), lax.axis_index("col")]).astype(jnp.int32)
    onward = [(c, (c + 1) % count) for c in range(count)]
    backward = [(c, (c - 1) % count) for c in range(count)]

    own_a, own_b = call(
        halves_kernel,
        out_shape=[shaped((cut, width)), shaped((size - cut, width))],
        in_specs=[HBM],
        out_specs=[VMEM] * 2,
        scratch_shapes=[pltpu.SemaphoreType.DMA((2,))],
        mib=4,
        cost=(0, 1 << 19),
    )(fixed(panel_y))
    left_a = lax.ppermute(own_a, "col", onward)
    right_b = lax.ppermute(own_b, "col", backward)
    left_b = lax.ppermute(own_b, "col", onward)
    right_a = lax.ppermute(own_a, "col", backward)
    opp_a = lax.ppermute(left_a, "col", onward)
    opp_b = lax.ppermute(right_b, "col", backward)

    square = shaped((width, width), BF16)
    mix = shaped((width, 2 * width), BF16)
    tall = shaped((rows, width), BF16)
    wide = shaped((width, rows), BF16)
    cube = 2 * 3 * width**3
    units, chunks = layout()
    th, tl, block = call(
        prepare_kernel,
        out_shape=[square, square, shaped((rows, units[0][1]))],
        in_specs=[HBM] * 2,
        out_specs=[VMEM] * 3,
        scratch_shapes=[pltpu.VMEM((width, width), F32), pltpu.SemaphoreType.DMA((2,))],
        mib=8,
        cost=(cube, 1 << 20),
    )(fixed(panel_t), fixed(trailing))

    w = units[0][1]
    partial, yh, yl, fh, fl = call(
        early_kernel,
        out_shape=[shaped((width, w)), tall, tall, wide, wide],
        in_specs=[SMEM] + [VMEM] * 7,
        out_specs=[VMEM] * 5,
        mib=16,
        cost=(2 * cube, 4 << 20),
    )(place, own_a, own_b, left_a, left_b, right_a, right_b, block)

    top, proj, gh, gl, *opposite = call(
        first_kernel,
        out_shape=[shaped((width, w))] * 2 + [square] * 6,
        in_specs=[SMEM] + [VMEM] * 8,
        out_specs=[VMEM] * 8,
        mib=16,
        cost=(2 * cube, 2 << 20),
    )(place, partial, opp_a, opp_b, block, th, tl, yh, yl)

    yh, yl, fh, fl = call(
        assemble_kernel,
        out_shape=[tall, tall, wide, wide],
        in_specs=[SMEM] + [VMEM] * 8,
        out_specs=[VMEM] * 4,
        mib=16,
        cost=(0, 4 << 20),
    )(place, yh, yl, fh, fl, *opposite)

    def swap(level, values):
        route = [(r, r ^ (1 << level)) for r in range(lax.axis_size("row"))]
        return lax.ppermute(values, "row", route)

    def combine(level, values, widths):
        w = values.shape[1]
        return call(
            level_kernel,
            out_shape=[shaped((width, w)) for w in widths],
            in_specs=[VMEM] * 4,
            out_specs=[VMEM] * len(widths),
            mib=8,
            cost=(2 * cube * w // width, 1 << 20),
        )(values, swap(level, values), *mixes[2 * level : 2 * level + 2])

    mixes = []

    def mix_matrices(level, after):
        mixes.extend(
            call(
                functools.partial(mixes_kernel, level),
                out_shape=[mix] * 2,
                in_specs=[SMEM] + [VMEM] * 2 + [ANY],
                out_specs=[VMEM] * 2,
                mib=8,
                cost=(2 * cube, 1 << 20),
            )(place, tree_v, tree_t, after)
        )

    tops, projs = [], []
    for u, (first, w) in enumerate(units):
        if u:
            top, proj = call(
                functools.partial(next_kernel, slice(first, first + w)),
                out_shape=[shaped((width, w))] * 2,
                in_specs=[VMEM] * 5,
                out_specs=[VMEM] * 2,
                mib=16,
                cost=(5 * cube * w // width, 2 << 20),
            )(trailing, fh, fl, gh, gl)
        projs.append(proj)
        if u < levels - 1:
            mix_matrices(u, proj)
        tops += combine(0, top, UNITS[u])

    for level in range(1, levels - 1):
        tops = [combine(level, top, (top.shape[1],))[0] for top in tops]

    level = levels - 1
    mix_matrices(level, projs[-1])

    out = ()
    parts = rows // size - 1
    for group in ((0, 1), (2, 3)):
        first = units[group[0]][0]
        w = sum(units[u][1] for u in group)
        out = (
            call(
                functools.partial(rest_kernel, first),
                out_shape=shaped((rows, columns)),
                in_specs=[VMEM] * (5 + len(group)) + [HBM] * len(out),
                out_specs=HBM,
                scratch_shapes=[pltpu.VMEM((parts, size, w), F32), pltpu.SemaphoreType.DMA((parts,))],
                input_output_aliases={5 + len(group): 0} if out else {},
                mib=16,
                cost=(10 * cube, 4 << 20),
            )(trailing, yh, yl, th, tl, *[projs[u] for u in group], *out),
        )
    out = out[0]

    for k, (first, w) in enumerate(chunks):
        out = call(
            functools.partial(final_kernel, first),
            out_shape=shaped((rows, columns)),
            in_specs=[VMEM] * 4 + [HBM],
            out_specs=HBM,
            scratch_shapes=[pltpu.VMEM((width, w), F32), pltpu.SemaphoreType.DMA],
            input_output_aliases={4: 0},
            mib=8,
            cost=(2 * cube * w // width, 1 << 20),
        )(tops[k], swap(level, tops[k]), *mixes[2 * level :], out)
    return out


def solution(mesh):
    placed = (
        P("row", "col"),
        P(("row", "col"), None),
        P("row", None),
        P(None, "row", None),
        P(None, "row", None),
    )
    return jax.shard_map(
        update, mesh=mesh, in_specs=placed, out_specs=P("row", "col"), check_vma=False
    )
```

```python
import functools
import math

import jax
import jax.numpy as jnp
from jax import lax
from jax.experimental import pallas as pl
from jax.experimental.pallas import tpu as pltpu
from jax.sharding import PartitionSpec as P


UNITS = ((128,), (128, 128), (128, 256), (256,))
F32 = jnp.float32
BF16 = jnp.bfloat16
VMEM = pl.BlockSpec(memory_space=pltpu.VMEM)
SMEM = pl.BlockSpec(memory_space=pltpu.SMEM)
HBM = pl.BlockSpec(memory_space=pltpu.HBM)
ANY = pl.BlockSpec(memory_space=pl.ANY)


def split(values):
    high = values.astype(BF16)
    return high, (values - high.astype(F32)).astype(BF16)


def dot3(left, right):
    mul = functools.partial(jnp.dot, preferred_element_type=F32)
    return mul(left[0], right[0]) + (mul(left[0], right[1]) + mul(left[1], right[0]))


def grids(shape):
    return lax.broadcasted_iota(jnp.int32, shape, 0), lax.broadcasted_iota(jnp.int32, shape, 1)


def unit_lower(values, first_row):
    rows, cols = grids(values.shape)
    rows = rows + first_row
    return jnp.where(rows > cols, values, jnp.where(rows == cols, F32(1.0), F32(0.0)))


def triangle_factor(values):
    rows, cols = grids(values.shape)
    scale = 2.0 / math.sqrt(values.shape[-1])
    return jnp.where(rows == cols, values, jnp.where(cols > rows, (values - 1.0) * scale, F32(0.0)))


def upper_part(values):
    rows, cols = grids(values.shape)
    return jnp.where(cols >= rows, values, F32(0.0))


def mix_level(leads, tree_v, tree_t, high, low):
    width = tree_v.shape[0]
    vees = upper_part(tree_v)
    tees = split(triangle_factor(tree_t).T)

    @pl.when(leads)
    def _():
        high[:, :width], low[:, :width] = tees
        high[:, width:], low[:, width:] = split(dot3(tees, split(vees.T)))

    @pl.when(jnp.logical_not(leads))
    def _():
        both = split(dot3(split(vees), tees))
        high[:, width:], low[:, width:] = both
        high[:, :width], low[:, :width] = split(dot3(both, split(vees.T)))


def start_all(pairs, sems):
    copies = [pltpu.make_async_copy(a, b, sems.at[i]) for i, (a, b) in enumerate(pairs)]
    for copy in copies:
        copy.start()
    return copies


def prepare_kernel(place, panel_t, tree_v, tree_t, trailing, th, tl, high, low, block, tri, vee, tee, sems):
    piece = trailing.at[:, : block.shape[1]]
    copies = start_all(((panel_t, tri), (tree_v.at[0], vee), (tree_t.at[0], tee), (piece, block)), sems)
    copies[0].wait()
    th[...], tl[...] = split(triangle_factor(tri[...]).T)
    copies[1].wait()
    copies[2].wait()
    mix_level(place[0] & 1 == 0, vee[...], tee[...], high, low)
    copies[3].wait()


def mixes_kernel(level, place, tree_v, tree_t, after, high, low):
    del after
    mix_level((place[0] >> level) & 1 == 0, tree_v[level], tree_t[level], high, low)


def opposite_rows(col, size, count):
    return pl.multiple_of(lax.rem(col + count // 2, count) * size, size)


def both_ways(rows, start):
    rows = unit_lower(rows, start)
    return split(rows), split(rows.T)


def early_kernel(place, own_a, own_b, left_a, left_b, right_a, right_b, block, partial, yh, yl, fh, fl):
    col = place[1]
    size = own_a.shape[0] + own_b.shape[0]
    count = block.shape[0] // size
    width = partial.shape[1]
    total = None
    for shift, parts in ((0, (own_a, own_b)), (count - 1, (left_a, left_b)), (1, (right_a, right_b))):
        start = pl.multiple_of(lax.rem(col + shift, count) * size, size)
        rows = jnp.concatenate([p[...] for p in parts], axis=0)
        here = pl.ds(start, size)
        straight, flipped = both_ways(rows, start)
        yh[here, :], yl[here, :] = straight
        fh[:, here], fl[:, here] = flipped
        term = dot3(flipped, split(block[pl.ds(start, size), :width]))
        total = term if total is None else total + term
    partial[...] = total


def store_parts(value, parts):
    first = 0
    for part in parts:
        part[...] = value[:, first : first + part.shape[1]]
        first += part.shape[1]


def first_kernel(place, partial, opp_a, opp_b, block, th, tl, yh, yl, top, proj, gh, gl, oh, ol, ph, plow):
    size = opp_a.shape[0] + opp_b.shape[0]
    width = partial.shape[1]
    start = opposite_rows(place[1], size, block.shape[0] // size)
    rows = jnp.concatenate([opp_a[...], opp_b[...]], axis=0)
    straight, flipped = both_ways(rows, start)
    upper = [jnp.where(start == 0, new, old[:size, :]) for new, old in zip(straight, (yh, yl))]
    gain = split(dot3(upper, (th[...], tl[...])))
    value = partial[...] + dot3(flipped, split(block[pl.ds(start, size), :width]))
    top[...] = block[:size, :width] - dot3(gain, split(value))
    proj[...] = value
    gh[...], gl[...] = gain
    oh[...], ol[...] = straight
    ph[...], plow[...] = flipped


def assemble_kernel(place, yh_in, yl_in, fh_in, fl_in, oh, ol, ph, plow, yh, yl, fh, fl):
    size = oh.shape[0]
    here = pl.ds(opposite_rows(place[1], size, yh.shape[0] // size), size)
    for out, old, new in ((yh, yh_in, oh), (yl, yl_in, ol)):
        out[...] = old[...]
        out[here, :] = new[...]
    for out, old, new in ((fh, fh_in, ph), (fl, fl_in, plow)):
        out[...] = old[...]
        out[:, here] = new[...]


def next_kernel(span, block, fh, fl, gh, gl, top, proj):
    values = block[:, span]
    value = dot3((fh[...], fl[...]), split(values))
    top[...] = values[: top.shape[0]] - dot3((gh[...], gl[...]), split(value))
    proj[...] = value


def rest_kernel(first, block, yh, yl, th, tl, *args):
    projs, (out, slots, sems) = args[: -3 - (first > 0)], args[-3:]
    count, size, width = slots.shape
    weights = [split(dot3((th[...], tl[...]), split(proj[...]))) for proj in projs]
    copies = []
    for i in range(count):
        here = slice((i + 1) * size, (i + 2) * size)
        at = 0
        for weight in weights:
            wide = weight[0].shape[1]
            values = block[here, first + at : first + at + wide]
            slots[i, :, at : at + wide] = values - dot3((yh[here, :], yl[here, :]), weight)
            at += wide
        target = out.at[pl.ds((i + 1) * size, size), pl.ds(first, width)]
        copies.append(pltpu.make_async_copy(slots.at[i], target, sems.at[i]))
        copies[-1].start()
    for copy in copies:
        copy.wait()


def mixed(mine, theirs, high, low):
    width = mine.shape[0]
    one = dot3((high[:, :width], low[:, :width]), split(mine[...]))
    two = dot3((high[:, width:], low[:, width:]), split(theirs[...]))
    return mine[...] - (one + two)


def level_kernel(mine, theirs, high, low, *parts):
    store_parts(mixed(mine, theirs, high, low), parts)


def final_kernel(first, mine, theirs, high, low, whole, out, slot, sem):
    del whole
    slot[...] = mixed(mine, theirs, high, low)
    copy = pltpu.make_async_copy(slot, out.at[pl.ds(0, slot.shape[0]), pl.ds(first, slot.shape[1])], sem)
    copy.start()
    copy.wait()


def shaped(shape, dtype=F32):
    return jax.ShapeDtypeStruct(shape, dtype)


def layout():
    units, chunks, first = [], [], 0
    for unit in UNITS:
        units.append((first, sum(unit)))
        for w in unit:
            chunks.append((first, w))
            first += w
    return units, chunks


def call(kernel, **options):
    mib = options.pop("mib")
    flops, moved = options.pop("cost")
    return pl.pallas_call(
        kernel,
        compiler_params=pltpu.CompilerParams(vmem_limit_bytes=mib << 20),
        cost_estimate=pl.CostEstimate(flops=flops, bytes_accessed=moved, transcendentals=0),
        **options,
    )


def fixed(values):
    return pltpu.with_memory_space_constraint(values, pltpu.HBM)


def update(trailing, panel_y, panel_t, tree_v, tree_t):
    size, width = panel_y.shape
    rows, columns = trailing.shape
    levels = tree_v.shape[0]
    cut = size // 2
    count = lax.axis_size("col")
    place = jnp.stack([lax.axis_index("row"), lax.axis_index("col")]).astype(jnp.int32)
    onward = [(c, (c + 1) % count) for c in range(count)]
    backward = [(c, (c - 1) % count) for c in range(count)]

    own_a, own_b = panel_y[:cut], panel_y[cut:]
    left_a = lax.ppermute(own_a, "col", onward)
    right_b = lax.ppermute(own_b, "col", backward)
    left_b = lax.ppermute(own_b, "col", onward)
    right_a = lax.ppermute(own_a, "col", backward)
    opp_a = lax.ppermute(left_a, "col", onward)
    opp_b = lax.ppermute(right_b, "col", backward)

    square = shaped((width, width), BF16)
    mix = shaped((width, 2 * width), BF16)
    tall = shaped((rows, width), BF16)
    wide = shaped((width, rows), BF16)
    cube = 2 * 3 * width**3
    units, chunks = layout()
    th, tl, *mixes, block = call(
        prepare_kernel,
        out_shape=[square, square, mix, mix, shaped((rows, units[0][1]))],
        in_specs=[SMEM] + [HBM] * 4,
        out_specs=[VMEM] * 5,
        scratch_shapes=[pltpu.VMEM((width, width), F32)] * 3 + [pltpu.SemaphoreType.DMA((4,))],
        mib=8,
        cost=(3 * cube, 1 << 20),
    )(place, fixed(panel_t), fixed(tree_v), fixed(tree_t), fixed(trailing))

    w = units[0][1]
    partial, yh, yl, fh, fl = call(
        early_kernel,
        out_shape=[shaped((width, w)), tall, tall, wide, wide],
        in_specs=[SMEM] + [VMEM] * 7,
        out_specs=[VMEM] * 5,
        mib=16,
        cost=(2 * cube, 4 << 20),
    )(place, own_a, own_b, left_a, left_b, right_a, right_b, block)

    top, proj, gh, gl, *opposite = call(
        first_kernel,
        out_shape=[shaped((width, w))] * 2 + [square] * 6,
        in_specs=[SMEM] + [VMEM] * 8,
        out_specs=[VMEM] * 8,
        mib=16,
        cost=(2 * cube, 2 << 20),
    )(place, partial, opp_a, opp_b, block, th, tl, yh, yl)

    yh, yl, fh, fl = call(
        assemble_kernel,
        out_shape=[tall, tall, wide, wide],
        in_specs=[SMEM] + [VMEM] * 8,
        out_specs=[VMEM] * 4,
        mib=16,
        cost=(0, 4 << 20),
    )(place, yh, yl, fh, fl, *opposite)

    def swap(level, values):
        route = [(r, r ^ (1 << level)) for r in range(lax.axis_size("row"))]
        return lax.ppermute(values, "row", route)

    def combine(level, values, widths):
        w = values.shape[1]
        return call(
            level_kernel,
            out_shape=[shaped((width, w)) for w in widths],
            in_specs=[VMEM] * 4,
            out_specs=[VMEM] * len(widths),
            mib=8,
            cost=(2 * cube * w // width, 1 << 20),
        )(values, swap(level, values), *mixes[2 * level : 2 * level + 2])

    def mix_matrices(level, after):
        mixes.extend(
            call(
                functools.partial(mixes_kernel, level),
                out_shape=[mix] * 2,
                in_specs=[SMEM] + [VMEM] * 2 + [ANY],
                out_specs=[VMEM] * 2,
                mib=8,
                cost=(2 * cube, 1 << 20),
            )(place, tree_v, tree_t, after)
        )

    tops, projs = [], []
    for u, (first, w) in enumerate(units):
        if u:
            top, proj = call(
                functools.partial(next_kernel, slice(first, first + w)),
                out_shape=[shaped((width, w))] * 2,
                in_specs=[VMEM] * 5,
                out_specs=[VMEM] * 2,
                mib=16,
                cost=(5 * cube * w // width, 2 << 20),
            )(trailing, fh, fl, gh, gl)
        projs.append(proj)
        if 0 < u < levels - 1:
            mix_matrices(u, proj)
        tops += combine(0, top, UNITS[u])

    for level in range(1, levels - 1):
        tops = [combine(level, top, (top.shape[1],))[0] for top in tops]

    level = levels - 1
    mix_matrices(level, projs[-1])

    out = ()
    parts = rows // size - 1
    for group in ((0, 1), (2, 3)):
        first = units[group[0]][0]
        w = sum(units[u][1] for u in group)
        out = (
            call(
                functools.partial(rest_kernel, first),
                out_shape=shaped((rows, columns)),
                in_specs=[VMEM] * (5 + len(group)) + [HBM] * len(out),
                out_specs=HBM,
                scratch_shapes=[pltpu.VMEM((parts, size, w), F32), pltpu.SemaphoreType.DMA((parts,))],
                input_output_aliases={5 + len(group): 0} if out else {},
                mib=16,
                cost=(10 * cube, 4 << 20),
            )(trailing, yh, yl, th, tl, *[projs[u] for u in group], *out),
        )
    out = out[0]

    for k, (first, w) in enumerate(chunks):
        out = call(
            functools.partial(final_kernel, first),
            out_shape=shaped((rows, columns)),
            in_specs=[VMEM] * 4 + [HBM],
            out_specs=HBM,
            scratch_shapes=[pltpu.VMEM((width, w), F32), pltpu.SemaphoreType.DMA],
            input_output_aliases={4: 0},
            mib=8,
            cost=(2 * cube * w // width, 1 << 20),
        )(tops[k], swap(level, tops[k]), *mixes[2 * level :], out)
    return out


def solution(mesh):
    placed = (
        P("row", "col"),
        P(("row", "col"), None),
        P("row", None),
        P(None, "row", None),
        P(None, "row", None),
    )
    return jax.shard_map(update, mesh=mesh, in_specs=placed, out_specs=P("row", "col"), check_vma=False)
```

```python
import functools
import math

import jax
import jax.numpy as jnp
from jax import lax
from jax.experimental import pallas as pl
from jax.experimental.pallas import tpu as pltpu
from jax.sharding import PartitionSpec as P


UNITS = ((128,), (128,), (128, 128), (256,), (128, 128))
STEPS = ((0, 1), (2,), (3,), (4,))
F32 = jnp.float32
BF16 = jnp.bfloat16
VMEM = pl.BlockSpec(memory_space=pltpu.VMEM)
SMEM = pl.BlockSpec(memory_space=pltpu.SMEM)
HBM = pl.BlockSpec(memory_space=pltpu.HBM)
ANY = pl.BlockSpec(memory_space=pl.ANY)


def split(values):
    high = values.astype(BF16)
    return high, (values - high.astype(F32)).astype(BF16)


def dot3(left, right):
    mul = functools.partial(jnp.dot, preferred_element_type=F32)
    return mul(left[0], right[0]) + (mul(left[0], right[1]) + mul(left[1], right[0]))


def grids(shape):
    return lax.broadcasted_iota(jnp.int32, shape, 0), lax.broadcasted_iota(jnp.int32, shape, 1)


def unit_lower(values, first_row):
    rows, cols = grids(values.shape)
    rows = rows + first_row
    return jnp.where(rows > cols, values, jnp.where(rows == cols, F32(1.0), F32(0.0)))


def triangle_factor(values):
    rows, cols = grids(values.shape)
    scale = 2.0 / math.sqrt(values.shape[-1])
    return jnp.where(rows == cols, values, jnp.where(cols > rows, (values - 1.0) * scale, F32(0.0)))


def upper_part(values):
    rows, cols = grids(values.shape)
    return jnp.where(cols >= rows, values, F32(0.0))


def mix_level(leads, tree_v, tree_t, high, low):
    width = tree_v.shape[0]
    vees = upper_part(tree_v)
    tees = split(triangle_factor(tree_t).T)

    @pl.when(leads)
    def _():
        high[:, :width], low[:, :width] = tees
        high[:, width:], low[:, width:] = split(dot3(tees, split(vees.T)))

    @pl.when(jnp.logical_not(leads))
    def _():
        both = split(dot3(split(vees), tees))
        high[:, width:], low[:, width:] = both
        high[:, :width], low[:, :width] = split(dot3(both, split(vees.T)))


def start_all(pairs, sems):
    copies = [pltpu.make_async_copy(a, b, sems.at[i]) for i, (a, b) in enumerate(pairs)]
    for copy in copies:
        copy.start()
    return copies


def prepare(place, panel_t, tree_v, tree_t, trailing, th, tl, high, low, block, tri, vee, tee, sems):
    piece = trailing.at[:, : block.shape[1]]
    copies = start_all(((panel_t, tri), (tree_v.at[0], vee), (tree_t.at[0], tee), (piece, block)), sems)
    copies[0].wait()
    th[...], tl[...] = split(triangle_factor(tri[...]).T)
    copies[1].wait()
    copies[2].wait()
    mix_level(place[0] & 1 == 0, vee[...], tee[...], high, low)
    copies[3].wait()


def odd_core():
    return lax.rem(lax.axis_index("row"), 2) == 1


def ahead_kernel(*args):
    pl.when(odd_core())(lambda: prepare(*args))


def prepare_kernel(*args):
    olds, inputs, rest = args[:5], args[5:10], args[10:]

    @pl.when(odd_core())
    def _():
        for old, out in zip(olds, rest[:5]):
            out[...] = old[...]

    pl.when(jnp.logical_not(odd_core()))(lambda: prepare(*inputs, *rest))


def mixes_kernel(level, place, tree_v, tree_t, after, high, low):
    del after
    mix_level((place[0] >> level) & 1 == 0, tree_v[level], tree_t[level], high, low)


def opposite_rows(col, size, count):
    return pl.multiple_of(lax.rem(col + count // 2, count) * size, size)


def both_ways(rows, start):
    rows = unit_lower(rows, start)
    return split(rows), split(rows.T)


def early_kernel(place, own_a, own_b, left_a, left_b, right_a, right_b, block, partial, yh, yl, fh, fl):
    col = place[1]
    size = own_a.shape[0] + own_b.shape[0]
    count = block.shape[0] // size
    width = partial.shape[1]
    total = None
    for shift, parts in ((0, (own_a, own_b)), (count - 1, (left_a, left_b)), (1, (right_a, right_b))):
        start = pl.multiple_of(lax.rem(col + shift, count) * size, size)
        rows = jnp.concatenate([p[...] for p in parts], axis=0)
        here = pl.ds(start, size)
        straight, flipped = both_ways(rows, start)
        yh[here, :], yl[here, :] = straight
        fh[:, here], fl[:, here] = flipped
        term = dot3(flipped, split(block[pl.ds(start, size), :width]))
        total = term if total is None else total + term
    partial[...] = total


def store_parts(value, parts):
    first = 0
    for part in parts:
        part[...] = value[:, first : first + part.shape[1]]
        first += part.shape[1]


def first_kernel(place, partial, opp_a, opp_b, block, th, tl, yh, yl, *outs):
    tops, (proj, gh, gl, oh, ol, ph, plow) = outs[:-7], outs[-7:]
    size = opp_a.shape[0] + opp_b.shape[0]
    width = partial.shape[1]
    start = opposite_rows(place[1], size, block.shape[0] // size)
    rows = jnp.concatenate([opp_a[...], opp_b[...]], axis=0)
    straight, flipped = both_ways(rows, start)
    upper = [jnp.where(start == 0, new, old[:size, :]) for new, old in zip(straight, (yh, yl))]
    gain = split(dot3(upper, (th[...], tl[...])))
    value = partial[...] + dot3(flipped, split(block[pl.ds(start, size), :width]))
    store_parts(block[:size, :width] - dot3(gain, split(value)), tops)
    proj[...] = value
    gh[...], gl[...] = gain
    oh[...], ol[...] = straight
    ph[...], plow[...] = flipped


def assemble_kernel(place, yh_in, yl_in, fh_in, fl_in, oh, ol, ph, plow, yh, yl, fh, fl):
    size = oh.shape[0]
    here = pl.ds(opposite_rows(place[1], size, yh.shape[0] // size), size)
    for out, old, new in ((yh, yh_in, oh), (yl, yl_in, ol)):
        out[...] = old[...]
        out[here, :] = new[...]
    for out, old, new in ((fh, fh_in, ph), (fl, fl_in, plow)):
        out[...] = old[...]
        out[:, here] = new[...]


def next_kernel(span, block, fh, fl, gh, gl, top, proj):
    values = block[:, span]
    value = dot3((fh[...], fl[...]), split(values))
    top[...] = values[: top.shape[0]] - dot3((gh[...], gl[...]), split(value))
    proj[...] = value


def rest_kernel(first, block, yh, yl, th, tl, *args):
    projs, (out, slots, sems) = args[: -3 - (first > 0)], args[-3:]
    count, size, width = slots.shape
    weights = [split(dot3((th[...], tl[...]), split(proj[...]))) for proj in projs]
    copies = []
    for i in range(count):
        here = slice((i + 1) * size, (i + 2) * size)
        at = 0
        for weight in weights:
            wide = weight[0].shape[1]
            values = block[here, first + at : first + at + wide]
            slots[i, :, at : at + wide] = values - dot3((yh[here, :], yl[here, :]), weight)
            at += wide
        target = out.at[pl.ds((i + 1) * size, size), pl.ds(first, width)]
        copies.append(pltpu.make_async_copy(slots.at[i], target, sems.at[i]))
        copies[-1].start()
    for copy in copies:
        copy.wait()


def mixed(mine, theirs, high, low):
    width = mine.shape[0]
    one = dot3((high[:, :width], low[:, :width]), split(mine[...]))
    two = dot3((high[:, width:], low[:, width:]), split(theirs[...]))
    return mine[...] - (one + two)


def level_kernel(mine, theirs, high, low, *parts):
    store_parts(mixed(mine, theirs, high, low), parts)


def final_kernel(first, mine, theirs, high, low, whole, out, slot, sem):
    del whole
    slot[...] = mixed(mine, theirs, high, low)
    copy = pltpu.make_async_copy(slot, out.at[pl.ds(0, slot.shape[0]), pl.ds(first, slot.shape[1])], sem)
    copy.start()
    copy.wait()


def shaped(shape, dtype=F32):
    return jax.ShapeDtypeStruct(shape, dtype)


def layout():
    units, chunks, first = [], [], 0
    for unit in UNITS:
        units.append((first, sum(unit)))
        for w in unit:
            chunks.append((first, w))
            first += w
    return units, chunks


def call(kernel, **options):
    mib = options.pop("mib")
    flops, moved = options.pop("cost")
    return pl.pallas_call(
        kernel,
        compiler_params=pltpu.CompilerParams(vmem_limit_bytes=mib << 20),
        cost_estimate=pl.CostEstimate(flops=flops, bytes_accessed=moved, transcendentals=0),
        **options,
    )


def fixed(values):
    return pltpu.with_memory_space_constraint(values, pltpu.HBM)


def update(trailing, panel_y, panel_t, tree_v, tree_t):
    size, width = panel_y.shape
    rows, columns = trailing.shape
    levels = tree_v.shape[0]
    cut = size // 2
    count = lax.axis_size("col")
    place = jnp.stack([lax.axis_index("row"), lax.axis_index("col")]).astype(jnp.int32)
    onward = [(c, (c + 1) % count) for c in range(count)]
    backward = [(c, (c - 1) % count) for c in range(count)]

    own_a, own_b = panel_y[:cut], panel_y[cut:]
    left_a = lax.ppermute(own_a, "col", onward)
    right_b = lax.ppermute(own_b, "col", backward)
    left_b = lax.ppermute(own_b, "col", onward)
    right_a = lax.ppermute(own_a, "col", backward)
    opp_a = lax.ppermute(left_a, "col", onward)
    opp_b = lax.ppermute(right_b, "col", backward)

    square = shaped((width, width), BF16)
    mix = shaped((width, 2 * width), BF16)
    tall = shaped((rows, width), BF16)
    wide = shaped((width, rows), BF16)
    cube = 2 * 3 * width**3
    units, chunks = layout()
    steps = [(units[step[0]][0], sum(units[u][1] for u in step)) for step in STEPS]
    w = steps[0][1]
    sources = (place, fixed(panel_t), fixed(tree_v), fixed(tree_t), fixed(trailing))
    ready = [square, square, mix, mix, shaped((rows, w))]
    local = [pltpu.VMEM((width, width), F32)] * 3 + [pltpu.SemaphoreType.DMA((4,))]
    olds = call(
        ahead_kernel,
        out_shape=ready,
        in_specs=[SMEM] + [HBM] * 4,
        out_specs=[VMEM] * 5,
        scratch_shapes=local,
        mib=8,
        cost=(3 * cube, 1 << 20),
    )(*sources)
    th, tl, *mixes, block = call(
        prepare_kernel,
        out_shape=ready,
        in_specs=[VMEM] * 5 + [SMEM] + [HBM] * 4,
        out_specs=[VMEM] * 5,
        scratch_shapes=local,
        mib=8,
        cost=(3 * cube, 1 << 20),
    )(*olds, *sources)

    partial, yh, yl, fh, fl = call(
        early_kernel,
        out_shape=[shaped((width, w)), tall, tall, wide, wide],
        in_specs=[SMEM] + [VMEM] * 7,
        out_specs=[VMEM] * 5,
        mib=16,
        cost=(2 * cube, 4 << 20),
    )(place, own_a, own_b, left_a, left_b, right_a, right_b, block)

    outs = call(
        first_kernel,
        out_shape=[shaped((width, units[u][1])) for u in STEPS[0]] + [shaped((width, w))] + [square] * 6,
        in_specs=[SMEM] + [VMEM] * 8,
        out_specs=[VMEM] * (7 + len(STEPS[0])),
        mib=16,
        cost=(2 * cube, 2 << 20),
    )(place, partial, opp_a, opp_b, block, th, tl, yh, yl)
    raw, (proj, gh, gl, *opposite) = list(outs[:-7]), outs[-7:]
    projs = [proj]

    yh, yl, fh, fl = call(
        assemble_kernel,
        out_shape=[tall, tall, wide, wide],
        in_specs=[SMEM] + [VMEM] * 8,
        out_specs=[VMEM] * 4,
        mib=16,
        cost=(0, 4 << 20),
    )(place, yh, yl, fh, fl, *opposite)

    def swap(level, values):
        route = [(r, r ^ (1 << level)) for r in range(lax.axis_size("row"))]
        return lax.ppermute(values, "row", route)

    def combine(level, values, widths):
        w = values.shape[1]
        return call(
            level_kernel,
            out_shape=[shaped((width, w)) for w in widths],
            in_specs=[VMEM] * 4,
            out_specs=[VMEM] * len(widths),
            mib=8,
            cost=(2 * cube * w // width, 1 << 20),
        )(values, swap(level, values), *mixes[2 * level : 2 * level + 2])

    def mix_matrices(level, after):
        mixes.extend(
            call(
                functools.partial(mixes_kernel, level),
                out_shape=[mix] * 2,
                in_specs=[SMEM] + [VMEM] * 2 + [ANY],
                out_specs=[VMEM] * 2,
                mib=8,
                cost=(2 * cube, 1 << 20),
            )(place, tree_v, tree_t, after)
        )

    for k, (first, w) in enumerate(steps):
        if k:
            top, proj = call(
                functools.partial(next_kernel, slice(first, first + w)),
                out_shape=[shaped((width, w))] * 2,
                in_specs=[VMEM] * 5,
                out_specs=[VMEM] * 2,
                mib=16,
                cost=(5 * cube * w // width, 2 << 20),
            )(trailing, fh, fl, gh, gl)
            raw.append(top)
            projs.append(proj)
    for level in range(1, levels):
        mix_matrices(level, projs[0] if level < levels - 1 else projs[-1])
    tops = []
    for u, top in enumerate(raw):
        tops += combine(0, top, UNITS[u])

    for level in range(1, levels - 1):
        tops = [combine(level, top, (top.shape[1],))[0] for top in tops]

    level = levels - 1
    out = ()
    parts = rows // size - 1
    for group in ((0, 1), (2, 3)):
        first = steps[group[0]][0]
        w = sum(steps[k][1] for k in group)
        out = (
            call(
                functools.partial(rest_kernel, first),
                out_shape=shaped((rows, columns)),
                in_specs=[VMEM] * (5 + len(group)) + [HBM] * len(out),
                out_specs=HBM,
                scratch_shapes=[pltpu.VMEM((parts, size, w), F32), pltpu.SemaphoreType.DMA((parts,))],
                input_output_aliases={5 + len(group): 0} if out else {},
                mib=16,
                cost=(10 * cube, 4 << 20),
            )(trailing, yh, yl, th, tl, *[projs[k] for k in group], *out),
        )
    out = out[0]

    for k, (first, w) in enumerate(chunks):
        out = call(
            functools.partial(final_kernel, first),
            out_shape=shaped((rows, columns)),
            in_specs=[VMEM] * 4 + [HBM],
            out_specs=HBM,
            scratch_shapes=[pltpu.VMEM((width, w), F32), pltpu.SemaphoreType.DMA],
            input_output_aliases={4: 0},
            mib=8,
            cost=(2 * cube * w // width, 1 << 20),
        )(tops[k], swap(level, tops[k]), *mixes[2 * level :], out)
    return out


def solution(mesh):
    placed = (
        P("row", "col"),
        P(("row", "col"), None),
        P("row", None),
        P(None, "row", None),
        P(None, "row", None),
    )
    return jax.shard_map(update, mesh=mesh, in_specs=placed, out_specs=P("row", "col"), check_vma=False)
```

```python
import functools
import math

import jax
import jax.numpy as jnp
from jax import lax
from jax.experimental import pallas as pl
from jax.experimental.pallas import tpu as pltpu
from jax.sharding import PartitionSpec as P


UNITS = ((128,), (128,), (128, 128), (128, 128), (128, 128))
STEPS = ((0, 1), (2,), (3,), (4,))
F32 = jnp.float32
BF16 = jnp.bfloat16
VMEM = pl.BlockSpec(memory_space=pltpu.VMEM)
SMEM = pl.BlockSpec(memory_space=pltpu.SMEM)
HBM = pl.BlockSpec(memory_space=pltpu.HBM)
ANY = pl.BlockSpec(memory_space=pl.ANY)


def split(values):
    high = values.astype(BF16)
    return high, (values - high.astype(F32)).astype(BF16)


def dot3(left, right):
    mul = functools.partial(jnp.dot, preferred_element_type=F32)
    return mul(left[0], right[0]) + (mul(left[0], right[1]) + mul(left[1], right[0]))


def grids(shape):
    return lax.broadcasted_iota(jnp.int32, shape, 0), lax.broadcasted_iota(jnp.int32, shape, 1)


def unit_lower(values, first_row):
    rows, cols = grids(values.shape)
    rows = rows + first_row
    return jnp.where(rows > cols, values, jnp.where(rows == cols, F32(1.0), F32(0.0)))


def triangle_factor(values):
    rows, cols = grids(values.shape)
    scale = 2.0 / math.sqrt(values.shape[-1])
    return jnp.where(rows == cols, values, jnp.where(cols > rows, (values - 1.0) * scale, F32(0.0)))


def upper_part(values):
    rows, cols = grids(values.shape)
    return jnp.where(cols >= rows, values, F32(0.0))


def mix_level(leads, tree_v, tree_t, high, low):
    width = tree_v.shape[0]
    vees = upper_part(tree_v)
    tees = split(triangle_factor(tree_t).T)

    @pl.when(leads)
    def _():
        high[:, :width], low[:, :width] = tees
        high[:, width:], low[:, width:] = split(dot3(tees, split(vees.T)))

    @pl.when(jnp.logical_not(leads))
    def _():
        both = split(dot3(split(vees), tees))
        high[:, width:], low[:, width:] = both
        high[:, :width], low[:, :width] = split(dot3(both, split(vees.T)))


def start_all(pairs, sems):
    copies = [pltpu.make_async_copy(a, b, sems.at[i]) for i, (a, b) in enumerate(pairs)]
    for copy in copies:
        copy.start()
    return copies


def prepare_kernel(place, panel_t, tree_v, tree_t, trailing, th, tl, high, low, block, tri, vee, tee, sems):
    piece = trailing.at[:, : block.shape[1]]
    copies = start_all(((panel_t, tri), (tree_v.at[0], vee), (tree_t.at[0], tee), (piece, block)), sems)
    copies[0].wait()
    th[...], tl[...] = split(triangle_factor(tri[...]).T)
    copies[1].wait()
    copies[2].wait()
    mix_level(place[0] & 1 == 0, vee[...], tee[...], high, low)
    copies[3].wait()


def mixes_kernel(level, place, tree_v, tree_t, after, high, low):
    del after
    mix_level((place[0] >> level) & 1 == 0, tree_v[level], tree_t[level], high, low)


def opposite_rows(col, size, count):
    return pl.multiple_of(lax.rem(col + count // 2, count) * size, size)


def both_ways(rows, start):
    rows = unit_lower(rows, start)
    return split(rows), split(rows.T)


def early_kernel(place, own_a, own_b, left_a, left_b, right_a, right_b, block, partial, yh, yl, fh, fl):
    col = place[1]
    size = own_a.shape[0] + own_b.shape[0]
    count = block.shape[0] // size
    width = partial.shape[1]
    total = None
    for shift, parts in ((0, (own_a, own_b)), (count - 1, (left_a, left_b)), (1, (right_a, right_b))):
        start = pl.multiple_of(lax.rem(col + shift, count) * size, size)
        rows = jnp.concatenate([p[...] for p in parts], axis=0)
        here = pl.ds(start, size)
        straight, flipped = both_ways(rows, start)
        yh[here, :], yl[here, :] = straight
        fh[:, here], fl[:, here] = flipped
        term = dot3(flipped, split(block[pl.ds(start, size), :width]))
        total = term if total is None else total + term
    partial[...] = total


def store_parts(value, parts):
    first = 0
    for part in parts:
        part[...] = value[:, first : first + part.shape[1]]
        first += part.shape[1]


def first_kernel(place, partial, opp_a, opp_b, block, th, tl, yh, yl, *outs):
    tops, (proj, gh, gl, oh, ol, ph, plow) = outs[:-7], outs[-7:]
    size = opp_a.shape[0] + opp_b.shape[0]
    width = partial.shape[1]
    start = opposite_rows(place[1], size, block.shape[0] // size)
    rows = jnp.concatenate([opp_a[...], opp_b[...]], axis=0)
    straight, flipped = both_ways(rows, start)
    upper = [jnp.where(start == 0, new, old[:size, :]) for new, old in zip(straight, (yh, yl))]
    gain = split(dot3(upper, (th[...], tl[...])))
    value = partial[...] + dot3(flipped, split(block[pl.ds(start, size), :width]))
    store_parts(block[:size, :width] - dot3(gain, split(value)), tops)
    proj[...] = value
    gh[...], gl[...] = gain
    oh[...], ol[...] = straight
    ph[...], plow[...] = flipped


def assemble_kernel(place, yh_in, yl_in, fh_in, fl_in, oh, ol, ph, plow, yh, yl, fh, fl):
    size = oh.shape[0]
    here = pl.ds(opposite_rows(place[1], size, yh.shape[0] // size), size)
    for out, old, new in ((yh, yh_in, oh), (yl, yl_in, ol)):
        out[...] = old[...]
        out[here, :] = new[...]
    for out, old, new in ((fh, fh_in, ph), (fl, fl_in, plow)):
        out[...] = old[...]
        out[:, here] = new[...]


def next_kernel(span, block, fh, fl, gh, gl, top, proj):
    values = block[:, span]
    value = dot3((fh[...], fl[...]), split(values))
    top[...] = values[: top.shape[0]] - dot3((gh[...], gl[...]), split(value))
    proj[...] = value


def rest_kernel(first, block, yh, yl, th, tl, *args):
    projs, (out, slots, sems) = args[: -3 - (first > 0)], args[-3:]
    count, size, width = slots.shape
    weights = [split(dot3((th[...], tl[...]), split(proj[...]))) for proj in projs]
    copies = []
    for i in range(count):
        here = slice((i + 1) * size, (i + 2) * size)
        at = 0
        for weight in weights:
            wide = weight[0].shape[1]
            values = block[here, first + at : first + at + wide]
            slots[i, :, at : at + wide] = values - dot3((yh[here, :], yl[here, :]), weight)
            at += wide
        target = out.at[pl.ds((i + 1) * size, size), pl.ds(first, width)]
        copies.append(pltpu.make_async_copy(slots.at[i], target, sems.at[i]))
        copies[-1].start()
    for copy in copies:
        copy.wait()


def mixed(mine, theirs, high, low):
    width = mine.shape[0]
    one = dot3((high[:, :width], low[:, :width]), split(mine[...]))
    two = dot3((high[:, width:], low[:, width:]), split(theirs[...]))
    return mine[...] - (one + two)


def level_kernel(mine, theirs, high, low, *parts):
    store_parts(mixed(mine, theirs, high, low), parts)


def final_kernel(first, mine, theirs, high, low, whole, out, slot, sem):
    del whole
    slot[...] = mixed(mine, theirs, high, low)
    copy = pltpu.make_async_copy(slot, out.at[pl.ds(0, slot.shape[0]), pl.ds(first, slot.shape[1])], sem)
    copy.start()
    copy.wait()


def shaped(shape, dtype=F32):
    return jax.ShapeDtypeStruct(shape, dtype)


def layout():
    units, chunks, first = [], [], 0
    for unit in UNITS:
        units.append((first, sum(unit)))
        for w in unit:
            chunks.append((first, w))
            first += w
    return units, chunks


def call(kernel, **options):
    mib = options.pop("mib")
    flops, moved = options.pop("cost")
    return pl.pallas_call(
        kernel,
        compiler_params=pltpu.CompilerParams(vmem_limit_bytes=mib << 20),
        cost_estimate=pl.CostEstimate(flops=flops, bytes_accessed=moved, transcendentals=0),
        **options,
    )


def fixed(values):
    return pltpu.with_memory_space_constraint(values, pltpu.HBM)


def update(trailing, panel_y, panel_t, tree_v, tree_t):
    size, width = panel_y.shape
    rows, columns = trailing.shape
    levels = tree_v.shape[0]
    cut = size // 2
    count = lax.axis_size("col")
    place = jnp.stack([lax.axis_index("row"), lax.axis_index("col")]).astype(jnp.int32)
    onward = [(c, (c + 1) % count) for c in range(count)]
    backward = [(c, (c - 1) % count) for c in range(count)]

    own_a, own_b = panel_y[:cut], panel_y[cut:]
    left_a = lax.ppermute(own_a, "col", onward)
    right_b = lax.ppermute(own_b, "col", backward)
    left_b = lax.ppermute(own_b, "col", onward)
    right_a = lax.ppermute(own_a, "col", backward)
    opp_a = lax.ppermute(left_a, "col", onward)
    opp_b = lax.ppermute(right_b, "col", backward)

    square = shaped((width, width), BF16)
    mix = shaped((width, 2 * width), BF16)
    tall = shaped((rows, width), BF16)
    wide = shaped((width, rows), BF16)
    cube = 2 * 3 * width**3
    units, chunks = layout()
    steps = [(units[step[0]][0], sum(units[u][1] for u in step)) for step in STEPS]
    w = steps[0][1]
    th, tl, *mixes, block = call(
        prepare_kernel,
        out_shape=[square, square, mix, mix, shaped((rows, w))],
        in_specs=[SMEM] + [HBM] * 4,
        out_specs=[VMEM] * 5,
        scratch_shapes=[pltpu.VMEM((width, width), F32)] * 3 + [pltpu.SemaphoreType.DMA((4,))],
        mib=8,
        cost=(3 * cube, 1 << 20),
    )(place, fixed(panel_t), fixed(tree_v), fixed(tree_t), fixed(trailing))

    partial, yh, yl, fh, fl = call(
        early_kernel,
        out_shape=[shaped((width, w)), tall, tall, wide, wide],
        in_specs=[SMEM] + [VMEM] * 7,
        out_specs=[VMEM] * 5,
        mib=16,
        cost=(2 * cube, 4 << 20),
    )(place, own_a, own_b, left_a, left_b, right_a, right_b, block)

    outs = call(
        first_kernel,
        out_shape=[shaped((width, units[u][1])) for u in STEPS[0]] + [shaped((width, w))] + [square] * 6,
        in_specs=[SMEM] + [VMEM] * 8,
        out_specs=[VMEM] * (7 + len(STEPS[0])),
        mib=16,
        cost=(2 * cube, 2 << 20),
    )(place, partial, opp_a, opp_b, block, th, tl, yh, yl)
    raw, (proj, gh, gl, *opposite) = list(outs[:-7]), outs[-7:]
    projs = [proj]

    yh, yl, fh, fl = call(
        assemble_kernel,
        out_shape=[tall, tall, wide, wide],
        in_specs=[SMEM] + [VMEM] * 8,
        out_specs=[VMEM] * 4,
        mib=16,
        cost=(0, 4 << 20),
    )(place, yh, yl, fh, fl, *opposite)

    def swap(level, values):
        route = [(r, r ^ (1 << level)) for r in range(lax.axis_size("row"))]
        return lax.ppermute(values, "row", route)

    def combine(level, values, widths):
        w = values.shape[1]
        return call(
            level_kernel,
            out_shape=[shaped((width, w)) for w in widths],
            in_specs=[VMEM] * 4,
            out_specs=[VMEM] * len(widths),
            mib=8,
            cost=(2 * cube * w // width, 1 << 20),
        )(values, swap(level, values), *mixes[2 * level : 2 * level + 2])

    def mix_matrices(level, after):
        mixes.extend(
            call(
                functools.partial(mixes_kernel, level),
                out_shape=[mix] * 2,
                in_specs=[SMEM] + [VMEM] * 2 + [ANY],
                out_specs=[VMEM] * 2,
                mib=8,
                cost=(2 * cube, 1 << 20),
            )(place, tree_v, tree_t, after)
        )

    for k, (first, w) in enumerate(steps):
        if k:
            top, proj = call(
                functools.partial(next_kernel, slice(first, first + w)),
                out_shape=[shaped((width, w))] * 2,
                in_specs=[VMEM] * 5,
                out_specs=[VMEM] * 2,
                mib=16,
                cost=(5 * cube * w // width, 2 << 20),
            )(trailing, fh, fl, gh, gl)
            raw.append(top)
            projs.append(proj)
    for level in range(1, levels):
        mix_matrices(level, projs[0] if level < levels - 1 else projs[-1])
    tops = []
    for u, top in enumerate(raw):
        tops += combine(0, top, UNITS[u])

    for level in range(1, levels - 1):
        tops = [combine(level, top, (top.shape[1],))[0] for top in tops]

    level = levels - 1
    out = ()
    parts = rows // size - 1
    for group in ((0, 1), (2, 3)):
        first = steps[group[0]][0]
        w = sum(steps[k][1] for k in group)
        out = (
            call(
                functools.partial(rest_kernel, first),
                out_shape=shaped((rows, columns)),
                in_specs=[VMEM] * (5 + len(group)) + [HBM] * len(out),
                out_specs=HBM,
                scratch_shapes=[pltpu.VMEM((parts, size, w), F32), pltpu.SemaphoreType.DMA((parts,))],
                input_output_aliases={5 + len(group): 0} if out else {},
                mib=16,
                cost=(10 * cube, 4 << 20),
            )(trailing, yh, yl, th, tl, *[projs[k] for k in group], *out),
        )
    out = out[0]

    for k, (first, w) in enumerate(chunks):
        out = call(
            functools.partial(final_kernel, first),
            out_shape=shaped((rows, columns)),
            in_specs=[VMEM] * 4 + [HBM],
            out_specs=HBM,
            scratch_shapes=[pltpu.VMEM((width, w), F32), pltpu.SemaphoreType.DMA],
            input_output_aliases={4: 0},
            mib=8,
            cost=(2 * cube * w // width, 1 << 20),
        )(tops[k], swap(level, tops[k]), *mixes[2 * level :], out)
    return out


def solution(mesh):
    placed = (
        P("row", "col"),
        P(("row", "col"), None),
        P("row", None),
        P(None, "row", None),
        P(None, "row", None),
    )
    return jax.shard_map(update, mesh=mesh, in_specs=placed, out_specs=P("row", "col"), check_vma=False)
```

```python
import functools
import math

import jax
import jax.numpy as jnp
from jax import lax
from jax.experimental import pallas as pl
from jax.experimental.pallas import tpu as pltpu
from jax.sharding import PartitionSpec as P


UNITS = ((128,), (128,), (128, 128), (128, 128), (128, 128))
STEPS = ((0, 1), (2,), (3,), (4,))
ENDS = ((0, 1, 2, 3), (4, 5), (6,), (7,))
F32 = jnp.float32
BF16 = jnp.bfloat16
VMEM = pl.BlockSpec(memory_space=pltpu.VMEM)
SMEM = pl.BlockSpec(memory_space=pltpu.SMEM)
HBM = pl.BlockSpec(memory_space=pltpu.HBM)
ANY = pl.BlockSpec(memory_space=pl.ANY)


def split(values):
    high = values.astype(BF16)
    return high, (values - high.astype(F32)).astype(BF16)


def dot3(left, right):
    mul = functools.partial(jnp.dot, preferred_element_type=F32)
    return mul(left[0], right[0]) + (mul(left[0], right[1]) + mul(left[1], right[0]))


def grids(shape):
    return lax.broadcasted_iota(jnp.int32, shape, 0), lax.broadcasted_iota(jnp.int32, shape, 1)


def unit_lower(values, first_row):
    rows, cols = grids(values.shape)
    rows = rows + first_row
    return jnp.where(rows > cols, values, jnp.where(rows == cols, F32(1.0), F32(0.0)))


def triangle_factor(values):
    rows, cols = grids(values.shape)
    scale = 2.0 / math.sqrt(values.shape[-1])
    return jnp.where(rows == cols, values, jnp.where(cols > rows, (values - 1.0) * scale, F32(0.0)))


def upper_part(values):
    rows, cols = grids(values.shape)
    return jnp.where(cols >= rows, values, F32(0.0))


def mix_level(leads, tree_v, tree_t, high, low):
    width = tree_v.shape[0]
    vees = upper_part(tree_v)
    tees = split(triangle_factor(tree_t).T)

    @pl.when(leads)
    def _():
        high[:, :width], low[:, :width] = tees
        high[:, width:], low[:, width:] = split(dot3(tees, split(vees.T)))

    @pl.when(jnp.logical_not(leads))
    def _():
        both = split(dot3(split(vees), tees))
        high[:, width:], low[:, width:] = both
        high[:, :width], low[:, :width] = split(dot3(both, split(vees.T)))


def start_all(pairs, sems):
    copies = [pltpu.make_async_copy(a, b, sems.at[i]) for i, (a, b) in enumerate(pairs)]
    for copy in copies:
        copy.start()
    return copies


def prepare_kernel(place, panel_t, tree_v, tree_t, trailing, th, tl, high, low, block, tri, vee, tee, sems):
    piece = trailing.at[:, : block.shape[1]]
    copies = start_all(((panel_t, tri), (tree_v.at[0], vee), (tree_t.at[0], tee), (piece, block)), sems)
    copies[0].wait()
    th[...], tl[...] = split(triangle_factor(tri[...]).T)
    copies[1].wait()
    copies[2].wait()
    mix_level(place[0] & 1 == 0, vee[...], tee[...], high, low)
    copies[3].wait()


def mixes_kernel(level, place, tree_v, tree_t, after, high, low):
    del after
    mix_level((place[0] >> level) & 1 == 0, tree_v[level], tree_t[level], high, low)


def opposite_rows(col, size, count):
    return pl.multiple_of(lax.rem(col + count // 2, count) * size, size)


def both_ways(rows, start):
    rows = unit_lower(rows, start)
    return split(rows), split(rows.T)


def early_kernel(place, own_a, own_b, left_a, left_b, right_a, right_b, block, th, tl, partial, gh, gl, yh, yl, fh, fl):
    col = place[1]
    size = own_a.shape[0] + own_b.shape[0]
    count = block.shape[0] // size
    width = partial.shape[1]
    total = None
    for shift, parts in ((0, (own_a, own_b)), (count - 1, (left_a, left_b)), (1, (right_a, right_b))):
        start = pl.multiple_of(lax.rem(col + shift, count) * size, size)
        rows = jnp.concatenate([p[...] for p in parts], axis=0)
        here = pl.ds(start, size)
        straight, flipped = both_ways(rows, start)
        yh[here, :], yl[here, :] = straight
        fh[:, here], fl[:, here] = flipped
        term = dot3(flipped, split(block[pl.ds(start, size), :width]))
        total = term if total is None else total + term
    partial[...] = total

    @pl.when(lax.rem(col + count // 2, count) != 0)
    def _():
        gh[...], gl[...] = split(dot3((yh[:size, :], yl[:size, :]), (th[...], tl[...])))


def store_parts(value, parts):
    first = 0
    for part in parts:
        part[...] = value[:, first : first + part.shape[1]]
        first += part.shape[1]


def first_kernel(place, partial, opp_a, opp_b, block, th, tl, old_gh, old_gl, *outs):
    tops, (proj, gh, gl, oh, ol, ph, plow) = outs[:-7], outs[-7:]
    size = opp_a.shape[0] + opp_b.shape[0]
    width = partial.shape[1]
    start = opposite_rows(place[1], size, block.shape[0] // size)
    rows = jnp.concatenate([opp_a[...], opp_b[...]], axis=0)
    straight, flipped = both_ways(rows, start)

    @pl.when(start == 0)
    def _():
        gh[...], gl[...] = split(dot3(straight, (th[...], tl[...])))

    @pl.when(start != 0)
    def _():
        gh[...], gl[...] = old_gh[...], old_gl[...]

    value = partial[...] + dot3(flipped, split(block[pl.ds(start, size), :width]))
    store_parts(block[:size, :width] - dot3((gh[...], gl[...]), split(value)), tops)
    proj[...] = value
    oh[...], ol[...] = straight
    ph[...], plow[...] = flipped


def assemble_kernel(place, yh_in, yl_in, fh_in, fl_in, oh, ol, ph, plow, yh, yl, fh, fl):
    size = oh.shape[0]
    here = pl.ds(opposite_rows(place[1], size, yh.shape[0] // size), size)
    for out, old, new in ((yh, yh_in, oh), (yl, yl_in, ol)):
        out[...] = old[...]
        out[here, :] = new[...]
    for out, old, new in ((fh, fh_in, ph), (fl, fl_in, plow)):
        out[...] = old[...]
        out[:, here] = new[...]


def next_kernel(span, block, fh, fl, gh, gl, top, proj):
    values = block[:, span]
    value = dot3((fh[...], fl[...]), split(values))
    top[...] = values[: top.shape[0]] - dot3((gh[...], gl[...]), split(value))
    proj[...] = value


def rest_kernel(first, block, yh, yl, th, tl, *args):
    projs, (out, slots, sems) = args[: -3 - (first > 0)], args[-3:]
    count, size, width = slots.shape
    weights = [split(dot3((th[...], tl[...]), split(proj[...]))) for proj in projs]
    copies = []
    for i in range(count):
        here = slice((i + 1) * size, (i + 2) * size)
        at = 0
        for weight in weights:
            wide = weight[0].shape[1]
            values = block[here, first + at : first + at + wide]
            slots[i, :, at : at + wide] = values - dot3((yh[here, :], yl[here, :]), weight)
            at += wide
        target = out.at[pl.ds((i + 1) * size, size), pl.ds(first, width)]
        copies.append(pltpu.make_async_copy(slots.at[i], target, sems.at[i]))
        copies[-1].start()
    for copy in copies:
        copy.wait()


def mixed(mine, theirs, high, low):
    width = mine.shape[0]
    one = dot3((high[:, :width], low[:, :width]), split(mine[...]))
    two = dot3((high[:, width:], low[:, width:]), split(theirs[...]))
    return mine[...] - (one + two)


def level_kernel(mine, theirs, high, low, *parts):
    store_parts(mixed(mine, theirs, high, low), parts)


def final_kernel(first, count, high, low, *args):
    pieces, (out, slots, sems) = args[: 2 * count], args[-3:]
    half, w = slots.shape[2:]
    copies = []
    for k in range(count):
        mine, theirs = pieces[2 * k : 2 * k + 2]
        both = split(jnp.concatenate([mine[...], theirs[...]], axis=0))
        for i in range(2):
            rows = slice(i * half, (i + 1) * half)
            slots[k, i] = mine[rows, :] - dot3((high[rows, :], low[rows, :]), both)
            target = out.at[pl.ds(i * half, half), pl.ds(first + k * w, w)]
            copies.append(pltpu.make_async_copy(slots.at[k, i], target, sems.at[k, i]))
            copies[-1].start()
    for copy in copies:
        copy.wait()


def shaped(shape, dtype=F32):
    return jax.ShapeDtypeStruct(shape, dtype)


def layout():
    units, chunks, first = [], [], 0
    for unit in UNITS:
        units.append((first, sum(unit)))
        for w in unit:
            chunks.append((first, w))
            first += w
    return units, chunks


def call(kernel, **options):
    mib = options.pop("mib")
    flops, moved = options.pop("cost")
    return pl.pallas_call(
        kernel,
        compiler_params=pltpu.CompilerParams(vmem_limit_bytes=mib << 20),
        cost_estimate=pl.CostEstimate(flops=flops, bytes_accessed=moved, transcendentals=0),
        **options,
    )


def fixed(values):
    return pltpu.with_memory_space_constraint(values, pltpu.HBM)


def update(trailing, panel_y, panel_t, tree_v, tree_t):
    size, width = panel_y.shape
    rows, columns = trailing.shape
    levels = tree_v.shape[0]
    cut = size // 2
    count = lax.axis_size("col")
    place = jnp.stack([lax.axis_index("row"), lax.axis_index("col")]).astype(jnp.int32)
    onward = [(c, (c + 1) % count) for c in range(count)]
    backward = [(c, (c - 1) % count) for c in range(count)]

    own_a, own_b = panel_y[:cut], panel_y[cut:]
    left_a = lax.ppermute(own_a, "col", onward)
    right_b = lax.ppermute(own_b, "col", backward)
    left_b = lax.ppermute(own_b, "col", onward)
    right_a = lax.ppermute(own_a, "col", backward)
    opp_a = lax.ppermute(left_a, "col", onward)
    opp_b = lax.ppermute(right_b, "col", backward)

    square = shaped((width, width), BF16)
    mix = shaped((width, 2 * width), BF16)
    tall = shaped((rows, width), BF16)
    wide = shaped((width, rows), BF16)
    cube = 2 * 3 * width**3
    units, chunks = layout()
    steps = [(units[step[0]][0], sum(units[u][1] for u in step)) for step in STEPS]
    w = steps[0][1]
    th, tl, *mixes, block = call(
        prepare_kernel,
        out_shape=[square, square, mix, mix, shaped((rows, w))],
        in_specs=[SMEM] + [HBM] * 4,
        out_specs=[VMEM] * 5,
        scratch_shapes=[pltpu.VMEM((width, width), F32)] * 3 + [pltpu.SemaphoreType.DMA((4,))],
        mib=8,
        cost=(3 * cube, 1 << 20),
    )(place, fixed(panel_t), fixed(tree_v), fixed(tree_t), fixed(trailing))

    partial, gh, gl, yh, yl, fh, fl = call(
        early_kernel,
        out_shape=[shaped((width, w)), square, square, tall, tall, wide, wide],
        in_specs=[SMEM] + [VMEM] * 9,
        out_specs=[VMEM] * 7,
        mib=16,
        cost=(2 * cube, 4 << 20),
    )(place, own_a, own_b, left_a, left_b, right_a, right_b, block, th, tl)

    outs = call(
        first_kernel,
        out_shape=[shaped((width, units[u][1])) for u in STEPS[0]] + [shaped((width, w))] + [square] * 6,
        in_specs=[SMEM] + [VMEM] * 8,
        out_specs=[VMEM] * (7 + len(STEPS[0])),
        mib=16,
        cost=(2 * cube, 2 << 20),
    )(place, partial, opp_a, opp_b, block, th, tl, gh, gl)
    raw, (proj, gh, gl, *opposite) = list(outs[:-7]), outs[-7:]
    projs = [proj]

    yh, yl, fh, fl = call(
        assemble_kernel,
        out_shape=[tall, tall, wide, wide],
        in_specs=[SMEM] + [VMEM] * 8,
        out_specs=[VMEM] * 4,
        mib=16,
        cost=(0, 4 << 20),
    )(place, yh, yl, fh, fl, *opposite)

    def swap(level, values):
        route = [(r, r ^ (1 << level)) for r in range(lax.axis_size("row"))]
        return lax.ppermute(values, "row", route)

    def combine(level, values, widths):
        w = values.shape[1]
        return call(
            level_kernel,
            out_shape=[shaped((width, w)) for w in widths],
            in_specs=[VMEM] * 4,
            out_specs=[VMEM] * len(widths),
            mib=8,
            cost=(2 * cube * w // width, 1 << 20),
        )(values, swap(level, values), *mixes[2 * level : 2 * level + 2])

    def mix_matrices(level, after):
        mixes.extend(
            call(
                functools.partial(mixes_kernel, level),
                out_shape=[mix] * 2,
                in_specs=[SMEM] + [VMEM] * 2 + [ANY],
                out_specs=[VMEM] * 2,
                mib=8,
                cost=(2 * cube, 1 << 20),
            )(place, tree_v, tree_t, after)
        )

    for k, (first, w) in enumerate(steps):
        if k:
            top, proj = call(
                functools.partial(next_kernel, slice(first, first + w)),
                out_shape=[shaped((width, w))] * 2,
                in_specs=[VMEM] * 5,
                out_specs=[VMEM] * 2,
                mib=16,
                cost=(5 * cube * w // width, 2 << 20),
            )(trailing, fh, fl, gh, gl)
            raw.append(top)
            projs.append(proj)
    for level in range(1, levels):
        mix_matrices(level, projs[0] if level < levels - 1 else projs[-1])
    tops = []
    for u, top in enumerate(raw):
        tops += combine(0, top, UNITS[u])

    for level in range(1, levels - 1):
        tops = [combine(level, top, (top.shape[1],))[0] for top in tops]

    level = levels - 1
    out = ()
    parts = rows // size - 1
    for group in ((0, 1), (2, 3)):
        first = steps[group[0]][0]
        w = sum(steps[k][1] for k in group)
        out = (
            call(
                functools.partial(rest_kernel, first),
                out_shape=shaped((rows, columns)),
                in_specs=[VMEM] * (5 + len(group)) + [HBM] * len(out),
                out_specs=HBM,
                scratch_shapes=[pltpu.VMEM((parts, size, w), F32), pltpu.SemaphoreType.DMA((parts,))],
                input_output_aliases={5 + len(group): 0} if out else {},
                mib=16,
                cost=(10 * cube, 4 << 20),
            )(trailing, yh, yl, th, tl, *[projs[k] for k in group], *out),
        )
    out = out[0]

    for group in ENDS:
        first, w = chunks[group[0]]
        n = len(group)
        pieces = []
        for k in group:
            pieces += [tops[k], swap(level, tops[k])]
        out = call(
            functools.partial(final_kernel, first, n),
            out_shape=shaped((rows, columns)),
            in_specs=[VMEM] * (2 + 2 * n) + [HBM],
            out_specs=HBM,
            scratch_shapes=[pltpu.VMEM((n, 2, width // 2, w), F32), pltpu.SemaphoreType.DMA((n, 2))],
            input_output_aliases={2 + 2 * n: 0},
            mib=8,
            cost=(2 * cube * n * w // width, 1 << 20),
        )(*mixes[2 * level :], *pieces, out)
    return out


def solution(mesh):
    placed = (
        P("row", "col"),
        P(("row", "col"), None),
        P("row", None),
        P(None, "row", None),
        P(None, "row", None),
    )
    return jax.shard_map(update, mesh=mesh, in_specs=placed, out_specs=P("row", "col"), check_vma=False)
```

```python
import functools
import math

import jax
import jax.numpy as jnp
from jax import lax
from jax.experimental import pallas as pl
from jax.experimental.pallas import tpu as pltpu
from jax.sharding import PartitionSpec as P


UNITS = ((128,), (128,), (128, 128), (128, 128), (128, 128))
STEPS = ((0, 1), (2,), (3,), (4,))
ENDS = ((0, 1, 2, 3), (4, 5), (6,), (7,))
F32 = jnp.float32
BF16 = jnp.bfloat16
VMEM = pl.BlockSpec(memory_space=pltpu.VMEM)
SMEM = pl.BlockSpec(memory_space=pltpu.SMEM)
HBM = pl.BlockSpec(memory_space=pltpu.HBM)
ANY = pl.BlockSpec(memory_space=pl.ANY)


def split(values):
    high = values.astype(BF16)
    return high, (values - high.astype(F32)).astype(BF16)


def dot3(left, right):
    mul = functools.partial(jnp.dot, preferred_element_type=F32)
    return mul(left[0], right[0]) + (mul(left[0], right[1]) + mul(left[1], right[0]))


def grids(shape):
    return lax.broadcasted_iota(jnp.int32, shape, 0), lax.broadcasted_iota(jnp.int32, shape, 1)


def unit_lower(values, first_row):
    rows, cols = grids(values.shape)
    rows = rows + first_row
    return jnp.where(rows > cols, values, jnp.where(rows == cols, F32(1.0), F32(0.0)))


def triangle_factor(values):
    rows, cols = grids(values.shape)
    scale = 2.0 / math.sqrt(values.shape[-1])
    return jnp.where(rows == cols, values, jnp.where(cols > rows, (values - 1.0) * scale, F32(0.0)))


def upper_part(values):
    rows, cols = grids(values.shape)
    return jnp.where(cols >= rows, values, F32(0.0))


def mix_level(leads, tree_v, tree_t, high, low):
    width = tree_v.shape[0]
    vees = upper_part(tree_v)
    tees = split(triangle_factor(tree_t).T)

    @pl.when(leads)
    def _():
        high[:, :width], low[:, :width] = tees
        high[:, width:], low[:, width:] = split(dot3(tees, split(vees.T)))

    @pl.when(jnp.logical_not(leads))
    def _():
        both = split(dot3(split(vees), tees))
        high[:, width:], low[:, width:] = both
        high[:, :width], low[:, :width] = split(dot3(both, split(vees.T)))


def start_all(pairs, sems):
    copies = [pltpu.make_async_copy(a, b, sems.at[i]) for i, (a, b) in enumerate(pairs)]
    for copy in copies:
        copy.start()
    return copies


def prepare_kernel(place, panel_t, tree_v, tree_t, trailing, th, tl, high, low, block, tri, vee, tee, sems):
    piece = trailing.at[:, : block.shape[1]]
    copies = start_all(((panel_t, tri), (tree_v.at[0], vee), (tree_t.at[0], tee), (piece, block)), sems)
    copies[0].wait()
    th[...], tl[...] = split(triangle_factor(tri[...]).T)
    copies[1].wait()
    copies[2].wait()
    mix_level(place[0] & 1 == 0, vee[...], tee[...], high, low)
    copies[3].wait()


def mixes_kernel(level, place, tree_v, tree_t, after, high, low):
    del after
    mix_level((place[0] >> level) & 1 == 0, tree_v[level], tree_t[level], high, low)


def opposite_rows(col, size, count):
    return pl.multiple_of(lax.rem(col + count // 2, count) * size, size)


def both_ways(rows, start):
    rows = unit_lower(rows, start)
    return split(rows), split(rows.T)


def early_kernel(place, own_a, own_b, behind_a, behind_b, before_a, before_b, block, partial, yh, yl, fh, fl):
    col = place[1]
    size = own_a.shape[0] + own_b.shape[0]
    count = block.shape[0] // size
    width = partial.shape[1]
    total = None
    behind = jnp.where(place[0] & 1 == 0, count - 1, 1)
    for shift, parts in ((0, (own_a, own_b)), (behind, (behind_a, behind_b)), (count - behind, (before_a, before_b))):
        start = pl.multiple_of(lax.rem(col + shift, count) * size, size)
        rows = jnp.concatenate([p[...] for p in parts], axis=0)
        here = pl.ds(start, size)
        straight, flipped = both_ways(rows, start)
        yh[here, :], yl[here, :] = straight
        fh[:, here], fl[:, here] = flipped
        term = dot3(flipped, split(block[pl.ds(start, size), :width]))
        total = term if total is None else total + term
    partial[...] = total


def store_parts(value, parts):
    first = 0
    for part in parts:
        part[...] = value[:, first : first + part.shape[1]]
        first += part.shape[1]


def first_kernel(place, partial, opp_a, opp_b, block, th, tl, yh, yl, *outs):
    tops, (proj, gh, gl, oh, ol, ph, plow) = outs[:-7], outs[-7:]
    size = opp_a.shape[0] + opp_b.shape[0]
    width = partial.shape[1]
    start = opposite_rows(place[1], size, block.shape[0] // size)
    rows = jnp.concatenate([opp_a[...], opp_b[...]], axis=0)
    straight, flipped = both_ways(rows, start)
    upper = [jnp.where(start == 0, new, old[:size, :]) for new, old in zip(straight, (yh, yl))]
    gain = split(dot3(upper, (th[...], tl[...])))
    value = partial[...] + dot3(flipped, split(block[pl.ds(start, size), :width]))
    store_parts(block[:size, :width] - dot3(gain, split(value)), tops)
    proj[...] = value
    gh[...], gl[...] = gain
    oh[...], ol[...] = straight
    ph[...], plow[...] = flipped


def assemble_kernel(place, yh_in, yl_in, fh_in, fl_in, oh, ol, ph, plow, yh, yl, fh, fl):
    size = oh.shape[0]
    here = pl.ds(opposite_rows(place[1], size, yh.shape[0] // size), size)
    for out, old, new in ((yh, yh_in, oh), (yl, yl_in, ol)):
        out[...] = old[...]
        out[here, :] = new[...]
    for out, old, new in ((fh, fh_in, ph), (fl, fl_in, plow)):
        out[...] = old[...]
        out[:, here] = new[...]


def next_kernel(span, block, fh, fl, gh, gl, top, proj):
    values = block[:, span]
    value = dot3((fh[...], fl[...]), split(values))
    top[...] = values[: top.shape[0]] - dot3((gh[...], gl[...]), split(value))
    proj[...] = value


def rest_kernel(first, block, yh, yl, th, tl, *args):
    projs, (out, slots, sems) = args[: -3 - (first > 0)], args[-3:]
    count, size, width = slots.shape
    weights = [split(dot3((th[...], tl[...]), split(proj[...]))) for proj in projs]
    copies = []
    for i in range(count):
        here = slice((i + 1) * size, (i + 2) * size)
        at = 0
        for weight in weights:
            wide = weight[0].shape[1]
            values = block[here, first + at : first + at + wide]
            slots[i, :, at : at + wide] = values - dot3((yh[here, :], yl[here, :]), weight)
            at += wide
        target = out.at[pl.ds((i + 1) * size, size), pl.ds(first, width)]
        copies.append(pltpu.make_async_copy(slots.at[i], target, sems.at[i]))
        copies[-1].start()
    for copy in copies:
        copy.wait()


def mixed(mine, theirs, high, low):
    width = mine.shape[0]
    one = dot3((high[:, :width], low[:, :width]), split(mine[...]))
    two = dot3((high[:, width:], low[:, width:]), split(theirs[...]))
    return mine[...] - (one + two)


def level_kernel(mine, theirs, high, low, *parts):
    store_parts(mixed(mine, theirs, high, low), parts)


def final_kernel(first, count, high, low, *args):
    pieces, (out, slots, sems) = args[: 2 * count], args[-3:]
    half, w = slots.shape[2:]
    copies = []
    for k in range(count):
        mine, theirs = pieces[2 * k : 2 * k + 2]
        both = split(jnp.concatenate([mine[...], theirs[...]], axis=0))
        for i in range(2):
            rows = slice(i * half, (i + 1) * half)
            slots[k, i] = mine[rows, :] - dot3((high[rows, :], low[rows, :]), both)
            target = out.at[pl.ds(i * half, half), pl.ds(first + k * w, w)]
            copies.append(pltpu.make_async_copy(slots.at[k, i], target, sems.at[k, i]))
            copies[-1].start()
    for copy in copies:
        copy.wait()


def shaped(shape, dtype=F32):
    return jax.ShapeDtypeStruct(shape, dtype)


def layout():
    units, chunks, first = [], [], 0
    for unit in UNITS:
        units.append((first, sum(unit)))
        for w in unit:
            chunks.append((first, w))
            first += w
    return units, chunks


def call(kernel, **options):
    mib = options.pop("mib")
    flops, moved = options.pop("cost")
    return pl.pallas_call(
        kernel,
        compiler_params=pltpu.CompilerParams(vmem_limit_bytes=mib << 20),
        cost_estimate=pl.CostEstimate(flops=flops, bytes_accessed=moved, transcendentals=0),
        **options,
    )


def fixed(values):
    return pltpu.with_memory_space_constraint(values, pltpu.HBM)


def update(trailing, panel_y, panel_t, tree_v, tree_t):
    size, width = panel_y.shape
    rows, columns = trailing.shape
    levels = tree_v.shape[0]
    count = lax.axis_size("col")
    place = jnp.stack([lax.axis_index("row"), lax.axis_index("col")]).astype(jnp.int32)
    own_a, own_b = panel_y[: size // 2], panel_y[size // 2 :]

    def ring(values, step):
        route = []
        for r in range(lax.axis_size("row")):
            for c in range(count):
                to = (c + (step if r % 2 == 0 else -step)) % count
                route.append((r * count + c, r * count + to))
        return lax.ppermute(values, ("row", "col"), route)

    behind_a = ring(own_a, 1)
    before_b = ring(own_b, -1)
    behind_b = ring(own_b, 1)
    before_a = ring(own_a, -1)
    opp_a = ring(behind_a, 1)
    opp_b = ring(before_b, -1)

    square = shaped((width, width), BF16)
    mix = shaped((width, 2 * width), BF16)
    tall = shaped((rows, width), BF16)
    wide = shaped((width, rows), BF16)
    cube = 2 * 3 * width**3
    units, chunks = layout()
    steps = [(units[step[0]][0], sum(units[u][1] for u in step)) for step in STEPS]
    w = steps[0][1]
    th, tl, *mixes, block = call(
        prepare_kernel,
        out_shape=[square, square, mix, mix, shaped((rows, w))],
        in_specs=[SMEM] + [HBM] * 4,
        out_specs=[VMEM] * 5,
        scratch_shapes=[pltpu.VMEM((width, width), F32)] * 3 + [pltpu.SemaphoreType.DMA((4,))],
        mib=8,
        cost=(3 * cube, 1 << 20),
    )(place, fixed(panel_t), fixed(tree_v), fixed(tree_t), fixed(trailing))

    partial, yh, yl, fh, fl = call(
        early_kernel,
        out_shape=[shaped((width, w)), tall, tall, wide, wide],
        in_specs=[SMEM] + [VMEM] * 7,
        out_specs=[VMEM] * 5,
        mib=16,
        cost=(2 * cube, 4 << 20),
    )(place, own_a, own_b, behind_a, behind_b, before_a, before_b, block)

    outs = call(
        first_kernel,
        out_shape=[shaped((width, units[u][1])) for u in STEPS[0]] + [shaped((width, w))] + [square] * 6,
        in_specs=[SMEM] + [VMEM] * 8,
        out_specs=[VMEM] * (7 + len(STEPS[0])),
        mib=16,
        cost=(2 * cube, 2 << 20),
    )(place, partial, opp_a, opp_b, block, th, tl, yh, yl)
    raw, (proj, gh, gl, *opposite) = list(outs[:-7]), outs[-7:]
    projs = [proj]

    yh, yl, fh, fl = call(
        assemble_kernel,
        out_shape=[tall, tall, wide, wide],
        in_specs=[SMEM] + [VMEM] * 8,
        out_specs=[VMEM] * 4,
        mib=16,
        cost=(0, 4 << 20),
    )(place, yh, yl, fh, fl, *opposite)

    def swap(level, values):
        route = [(r, r ^ (1 << level)) for r in range(lax.axis_size("row"))]
        return lax.ppermute(values, "row", route)

    def combine(level, values, widths):
        w = values.shape[1]
        return call(
            level_kernel,
            out_shape=[shaped((width, w)) for w in widths],
            in_specs=[VMEM] * 4,
            out_specs=[VMEM] * len(widths),
            mib=8,
            cost=(2 * cube * w // width, 1 << 20),
        )(values, swap(level, values), *mixes[2 * level : 2 * level + 2])

    def mix_matrices(level, after):
        mixes.extend(
            call(
                functools.partial(mixes_kernel, level),
                out_shape=[mix] * 2,
                in_specs=[SMEM] + [VMEM] * 2 + [ANY],
                out_specs=[VMEM] * 2,
                mib=8,
                cost=(2 * cube, 1 << 20),
            )(place, tree_v, tree_t, after)
        )

    for k, (first, w) in enumerate(steps):
        if k:
            top, proj = call(
                functools.partial(next_kernel, slice(first, first + w)),
                out_shape=[shaped((width, w))] * 2,
                in_specs=[VMEM] * 5,
                out_specs=[VMEM] * 2,
                mib=16,
                cost=(5 * cube * w // width, 2 << 20),
            )(trailing, fh, fl, gh, gl)
            raw.append(top)
            projs.append(proj)
    for level in range(1, levels):
        mix_matrices(level, projs[0] if level < levels - 1 else projs[-1])
    tops = []
    for u, top in enumerate(raw):
        tops += combine(0, top, UNITS[u])

    for level in range(1, levels - 1):
        tops = [combine(level, top, (top.shape[1],))[0] for top in tops]

    level = levels - 1
    out = ()
    parts = rows // size - 1
    for group in ((0, 1), (2, 3)):
        first = steps[group[0]][0]
        w = sum(steps[k][1] for k in group)
        out = (
            call(
                functools.partial(rest_kernel, first),
                out_shape=shaped((rows, columns)),
                in_specs=[VMEM] * (5 + len(group)) + [HBM] * len(out),
                out_specs=HBM,
                scratch_shapes=[pltpu.VMEM((parts, size, w), F32), pltpu.SemaphoreType.DMA((parts,))],
                input_output_aliases={5 + len(group): 0} if out else {},
                mib=16,
                cost=(10 * cube, 4 << 20),
            )(trailing, yh, yl, th, tl, *[projs[k] for k in group], *out),
        )
    out = out[0]

    for group in ENDS:
        first, w = chunks[group[0]]
        n = len(group)
        pieces = []
        for k in group:
            pieces += [tops[k], swap(level, tops[k])]
        out = call(
            functools.partial(final_kernel, first, n),
            out_shape=shaped((rows, columns)),
            in_specs=[VMEM] * (2 + 2 * n) + [HBM],
            out_specs=HBM,
            scratch_shapes=[pltpu.VMEM((n, 2, width // 2, w), F32), pltpu.SemaphoreType.DMA((n, 2))],
            input_output_aliases={2 + 2 * n: 0},
            mib=8,
            cost=(2 * cube * n * w // width, 1 << 20),
        )(*mixes[2 * level :], *pieces, out)
    return out


def solution(mesh):
    placed = (
        P("row", "col"),
        P(("row", "col"), None),
        P("row", None),
        P(None, "row", None),
        P(None, "row", None),
    )
    return jax.shard_map(update, mesh=mesh, in_specs=placed, out_specs=P("row", "col"), check_vma=False)
```

```python
import functools
import math

import jax
import jax.numpy as jnp
from jax import lax
from jax.experimental import pallas as pl
from jax.experimental.pallas import tpu as pltpu
from jax.sharding import PartitionSpec as P


UNITS = ((128,), (128,), (128, 128), (128, 128), (128, 128))
STEPS = ((0, 1), (2,), (3,), (4,))
ENDS = ((0, 1, 2, 3), (4, 5), (6,), (7,))
F32 = jnp.float32
BF16 = jnp.bfloat16
VMEM = pl.BlockSpec(memory_space=pltpu.VMEM)
SMEM = pl.BlockSpec(memory_space=pltpu.SMEM)
HBM = pl.BlockSpec(memory_space=pltpu.HBM)
ANY = pl.BlockSpec(memory_space=pl.ANY)


def split(values):
    high = values.astype(BF16)
    return high, (values - high.astype(F32)).astype(BF16)


def dot3(left, right):
    mul = functools.partial(jnp.dot, preferred_element_type=F32)
    return mul(left[0], right[0]) + (mul(left[0], right[1]) + mul(left[1], right[0]))


def grids(shape):
    return lax.broadcasted_iota(jnp.int32, shape, 0), lax.broadcasted_iota(jnp.int32, shape, 1)


def unit_lower(values, first_row):
    rows, cols = grids(values.shape)
    rows = rows + first_row
    return jnp.where(rows > cols, values, jnp.where(rows == cols, F32(1.0), F32(0.0)))


def triangle_factor(values):
    rows, cols = grids(values.shape)
    scale = 2.0 / math.sqrt(values.shape[-1])
    return jnp.where(rows == cols, values, jnp.where(cols > rows, (values - 1.0) * scale, F32(0.0)))


def upper_part(values):
    rows, cols = grids(values.shape)
    return jnp.where(cols >= rows, values, F32(0.0))


def mix_level(leads, tree_v, tree_t, high, low):
    width = tree_v.shape[0]
    vees = upper_part(tree_v)
    tees = split(triangle_factor(tree_t).T)

    @pl.when(leads)
    def _():
        high[:, :width], low[:, :width] = tees
        high[:, width:], low[:, width:] = split(dot3(tees, split(vees.T)))

    @pl.when(jnp.logical_not(leads))
    def _():
        both = split(dot3(split(vees), tees))
        high[:, width:], low[:, width:] = both
        high[:, :width], low[:, :width] = split(dot3(both, split(vees.T)))


def start_all(pairs, sems):
    copies = [pltpu.make_async_copy(a, b, sems.at[i]) for i, (a, b) in enumerate(pairs)]
    for copy in copies:
        copy.start()
    return copies


def prepare_kernel(place, panel_t, tree_v, tree_t, trailing, th, tl, high, low, block, tri, vee, tee, sems):
    piece = trailing.at[:, : block.shape[1]]
    copies = start_all(((panel_t, tri), (tree_v.at[0], vee), (tree_t.at[0], tee), (piece, block)), sems)
    copies[0].wait()
    th[...], tl[...] = split(triangle_factor(tri[...]).T)
    copies[1].wait()
    copies[2].wait()
    mix_level(place[0] & 1 == 0, vee[...], tee[...], high, low)
    copies[3].wait()


def mixes_kernel(level, place, tree_v, tree_t, after, high, low):
    del after
    mix_level((place[0] >> level) & 1 == 0, tree_v[level], tree_t[level], high, low)


def opposite_rows(col, size, count):
    return pl.multiple_of(lax.rem(col + count // 2, count) * size, size)


def both_ways(rows, start):
    rows = unit_lower(rows, start)
    return split(rows), split(rows.T)


def early_kernel(place, own, behind, before_a, before_b, block, partial, yh, yl, fh, fl):
    col = place[1]
    size = own.shape[0]
    count = block.shape[0] // size
    width = partial.shape[1]
    total = None
    back = jnp.where(place[0] & 1 == 0, count - 1, 1)
    for shift, parts in ((0, (own,)), (back, (behind,)), (count - back, (before_a, before_b))):
        start = pl.multiple_of(lax.rem(col + shift, count) * size, size)
        rows = parts[0][...] if len(parts) == 1 else jnp.concatenate([p[...] for p in parts], axis=0)
        here = pl.ds(start, size)
        straight, flipped = both_ways(rows, start)
        yh[here, :], yl[here, :] = straight
        fh[:, here], fl[:, here] = flipped
        term = dot3(flipped, split(block[pl.ds(start, size), :width]))
        total = term if total is None else total + term
    partial[...] = total


def store_parts(value, parts):
    first = 0
    for part in parts:
        part[...] = value[:, first : first + part.shape[1]]
        first += part.shape[1]


def first_kernel(place, partial, opp_a, opp_b, block, th, tl, yh, yl, *outs):
    tops, (proj, gh, gl, oh, ol, ph, plow) = outs[:-7], outs[-7:]
    size = opp_a.shape[0] + opp_b.shape[0]
    width = partial.shape[1]
    start = opposite_rows(place[1], size, block.shape[0] // size)
    rows = jnp.concatenate([opp_a[...], opp_b[...]], axis=0)
    straight, flipped = both_ways(rows, start)
    upper = [jnp.where(start == 0, new, old[:size, :]) for new, old in zip(straight, (yh, yl))]
    gain = split(dot3(upper, (th[...], tl[...])))
    value = partial[...] + dot3(flipped, split(block[pl.ds(start, size), :width]))
    store_parts(block[:size, :width] - dot3(gain, split(value)), tops)
    proj[...] = value
    gh[...], gl[...] = gain
    oh[...], ol[...] = straight
    ph[...], plow[...] = flipped


def assemble_kernel(place, yh_in, yl_in, fh_in, fl_in, oh, ol, ph, plow, yh, yl, fh, fl):
    size = oh.shape[0]
    here = pl.ds(opposite_rows(place[1], size, yh.shape[0] // size), size)
    for out, old, new in ((yh, yh_in, oh), (yl, yl_in, ol)):
        out[...] = old[...]
        out[here, :] = new[...]
    for out, old, new in ((fh, fh_in, ph), (fl, fl_in, plow)):
        out[...] = old[...]
        out[:, here] = new[...]


def next_kernel(span, block, fh, fl, gh, gl, top, proj):
    values = block[:, span]
    value = dot3((fh[...], fl[...]), split(values))
    top[...] = values[: top.shape[0]] - dot3((gh[...], gl[...]), split(value))
    proj[...] = value


def rest_kernel(first, block, yh, yl, th, tl, *args):
    projs, (out, slots, sems) = args[: -3 - (first > 0)], args[-3:]
    count, size, width = slots.shape
    weights = [split(dot3((th[...], tl[...]), split(proj[...]))) for proj in projs]
    copies = []
    for i in range(count):
        here = slice((i + 1) * size, (i + 2) * size)
        at = 0
        for weight in weights:
            wide = weight[0].shape[1]
            values = block[here, first + at : first + at + wide]
            slots[i, :, at : at + wide] = values - dot3((yh[here, :], yl[here, :]), weight)
            at += wide
        target = out.at[pl.ds((i + 1) * size, size), pl.ds(first, width)]
        copies.append(pltpu.make_async_copy(slots.at[i], target, sems.at[i]))
        copies[-1].start()
    for copy in copies:
        copy.wait()


def mixed(mine, theirs, high, low):
    width = mine.shape[0]
    one = dot3((high[:, :width], low[:, :width]), split(mine[...]))
    two = dot3((high[:, width:], low[:, width:]), split(theirs[...]))
    return mine[...] - (one + two)


def level_kernel(mine, theirs, high, low, *parts):
    store_parts(mixed(mine, theirs, high, low), parts)


def final_kernel(first, count, high, low, *args):
    pieces, (out, slots, sems) = args[: 2 * count], args[-3:]
    half, w = slots.shape[2:]
    copies = []
    for k in range(count):
        mine, theirs = pieces[2 * k : 2 * k + 2]
        both = split(jnp.concatenate([mine[...], theirs[...]], axis=0))
        for i in range(2):
            rows = slice(i * half, (i + 1) * half)
            slots[k, i] = mine[rows, :] - dot3((high[rows, :], low[rows, :]), both)
            target = out.at[pl.ds(i * half, half), pl.ds(first + k * w, w)]
            copies.append(pltpu.make_async_copy(slots.at[k, i], target, sems.at[k, i]))
            copies[-1].start()
    for copy in copies:
        copy.wait()


def shaped(shape, dtype=F32):
    return jax.ShapeDtypeStruct(shape, dtype)


def layout():
    units, chunks, first = [], [], 0
    for unit in UNITS:
        units.append((first, sum(unit)))
        for w in unit:
            chunks.append((first, w))
            first += w
    return units, chunks


def call(kernel, **options):
    mib = options.pop("mib")
    flops, moved = options.pop("cost")
    return pl.pallas_call(
        kernel,
        compiler_params=pltpu.CompilerParams(vmem_limit_bytes=mib << 20),
        cost_estimate=pl.CostEstimate(flops=flops, bytes_accessed=moved, transcendentals=0),
        **options,
    )


def fixed(values):
    return pltpu.with_memory_space_constraint(values, pltpu.HBM)


def update(trailing, panel_y, panel_t, tree_v, tree_t):
    size, width = panel_y.shape
    rows, columns = trailing.shape
    levels = tree_v.shape[0]
    count = lax.axis_size("col")
    place = jnp.stack([lax.axis_index("row"), lax.axis_index("col")]).astype(jnp.int32)
    own_a, own_b = panel_y[: size // 2], panel_y[size // 2 :]

    def ring(values, step):
        route = []
        for r in range(lax.axis_size("row")):
            for c in range(count):
                to = (c + (step if r % 2 == 0 else -step)) % count
                route.append((r * count + c, r * count + to))
        return lax.ppermute(values, ("row", "col"), route)

    behind = ring(panel_y, 1)
    before_b = ring(own_b, -1)
    before_a = ring(own_a, -1)
    opp_b = ring(before_b, -1)
    opp_a = ring(behind[: size // 2], 1)

    square = shaped((width, width), BF16)
    mix = shaped((width, 2 * width), BF16)
    tall = shaped((rows, width), BF16)
    wide = shaped((width, rows), BF16)
    cube = 2 * 3 * width**3
    units, chunks = layout()
    steps = [(units[step[0]][0], sum(units[u][1] for u in step)) for step in STEPS]
    w = steps[0][1]
    th, tl, *mixes, block = call(
        prepare_kernel,
        out_shape=[square, square, mix, mix, shaped((rows, w))],
        in_specs=[SMEM] + [HBM] * 4,
        out_specs=[VMEM] * 5,
        scratch_shapes=[pltpu.VMEM((width, width), F32)] * 3 + [pltpu.SemaphoreType.DMA((4,))],
        mib=8,
        cost=(3 * cube, 1 << 20),
    )(place, fixed(panel_t), fixed(tree_v), fixed(tree_t), fixed(trailing))

    partial, yh, yl, fh, fl = call(
        early_kernel,
        out_shape=[shaped((width, w)), tall, tall, wide, wide],
        in_specs=[SMEM] + [VMEM] * 5,
        out_specs=[VMEM] * 5,
        mib=16,
        cost=(2 * cube, 4 << 20),
    )(place, panel_y, behind, before_a, before_b, block)

    outs = call(
        first_kernel,
        out_shape=[shaped((width, units[u][1])) for u in STEPS[0]] + [shaped((width, w))] + [square] * 6,
        in_specs=[SMEM] + [VMEM] * 8,
        out_specs=[VMEM] * (7 + len(STEPS[0])),
        mib=16,
        cost=(2 * cube, 2 << 20),
    )(place, partial, opp_a, opp_b, block, th, tl, yh, yl)
    raw, (proj, gh, gl, *opposite) = list(outs[:-7]), outs[-7:]
    projs = [proj]

    yh, yl, fh, fl = call(
        assemble_kernel,
        out_shape=[tall, tall, wide, wide],
        in_specs=[SMEM] + [VMEM] * 8,
        out_specs=[VMEM] * 4,
        mib=16,
        cost=(0, 4 << 20),
    )(place, yh, yl, fh, fl, *opposite)

    def swap(level, values):
        route = [(r, r ^ (1 << level)) for r in range(lax.axis_size("row"))]
        return lax.ppermute(values, "row", route)

    def combine(level, values, widths):
        w = values.shape[1]
        return call(
            level_kernel,
            out_shape=[shaped((width, w)) for w in widths],
            in_specs=[VMEM] * 4,
            out_specs=[VMEM] * len(widths),
            mib=8,
            cost=(2 * cube * w // width, 1 << 20),
        )(values, swap(level, values), *mixes[2 * level : 2 * level + 2])

    def mix_matrices(level, after):
        mixes.extend(
            call(
                functools.partial(mixes_kernel, level),
                out_shape=[mix] * 2,
                in_specs=[SMEM] + [VMEM] * 2 + [ANY],
                out_specs=[VMEM] * 2,
                mib=8,
                cost=(2 * cube, 1 << 20),
            )(place, tree_v, tree_t, after)
        )

    for k, (first, w) in enumerate(steps):
        if k:
            top, proj = call(
                functools.partial(next_kernel, slice(first, first + w)),
                out_shape=[shaped((width, w))] * 2,
                in_specs=[VMEM] * 5,
                out_specs=[VMEM] * 2,
                mib=16,
                cost=(5 * cube * w // width, 2 << 20),
            )(trailing, fh, fl, gh, gl)
            raw.append(top)
            projs.append(proj)
    for level in range(1, levels):
        mix_matrices(level, projs[0] if level < levels - 1 else projs[-1])
    tops = []
    for u, top in enumerate(raw):
        tops += combine(0, top, UNITS[u])

    for level in range(1, levels - 1):
        tops = [combine(level, top, (top.shape[1],))[0] for top in tops]

    level = levels - 1
    out = ()
    parts = rows // size - 1
    for group in ((0, 1), (2, 3)):
        first = steps[group[0]][0]
        w = sum(steps[k][1] for k in group)
        out = (
            call(
                functools.partial(rest_kernel, first),
                out_shape=shaped((rows, columns)),
                in_specs=[VMEM] * (5 + len(group)) + [HBM] * len(out),
                out_specs=HBM,
                scratch_shapes=[pltpu.VMEM((parts, size, w), F32), pltpu.SemaphoreType.DMA((parts,))],
                input_output_aliases={5 + len(group): 0} if out else {},
                mib=16,
                cost=(10 * cube, 4 << 20),
            )(trailing, yh, yl, th, tl, *[projs[k] for k in group], *out),
        )
    out = out[0]

    for group in ENDS:
        first, w = chunks[group[0]]
        n = len(group)
        pieces = []
        for k in group:
            pieces += [tops[k], swap(level, tops[k])]
        out = call(
            functools.partial(final_kernel, first, n),
            out_shape=shaped((rows, columns)),
            in_specs=[VMEM] * (2 + 2 * n) + [HBM],
            out_specs=HBM,
            scratch_shapes=[pltpu.VMEM((n, 2, width // 2, w), F32), pltpu.SemaphoreType.DMA((n, 2))],
            input_output_aliases={2 + 2 * n: 0},
            mib=8,
            cost=(2 * cube * n * w // width, 1 << 20),
        )(*mixes[2 * level :], *pieces, out)
    return out


def solution(mesh):
    placed = (
        P("row", "col"),
        P(("row", "col"), None),
        P("row", None),
        P(None, "row", None),
        P(None, "row", None),
    )
    return jax.shard_map(update, mesh=mesh, in_specs=placed, out_specs=P("row", "col"), check_vma=False)
```

```python
import functools
import math

import jax
import jax.numpy as jnp
from jax import lax
from jax.experimental import pallas as pl
from jax.experimental.pallas import tpu as pltpu
from jax.sharding import PartitionSpec as P


UNITS = ((128,), (128,), (128, 128), (128, 128), (128, 128))
STEPS = ((0, 1), (2,), (3,), (4,))
ENDS = ((0, 1, 2, 3), (4, 5), (6,), (7,))
F32 = jnp.float32
BF16 = jnp.bfloat16
VMEM = pl.BlockSpec(memory_space=pltpu.VMEM)
SMEM = pl.BlockSpec(memory_space=pltpu.SMEM)
HBM = pl.BlockSpec(memory_space=pltpu.HBM)
ANY = pl.BlockSpec(memory_space=pl.ANY)


def split(values):
    high = values.astype(BF16)
    return high, (values - high.astype(F32)).astype(BF16)


def dot3(left, right):
    mul = functools.partial(jnp.dot, preferred_element_type=F32)
    return mul(left[0], right[0]) + (mul(left[0], right[1]) + mul(left[1], right[0]))


def grids(shape):
    return lax.broadcasted_iota(jnp.int32, shape, 0), lax.broadcasted_iota(jnp.int32, shape, 1)


def unit_lower(values, first_row):
    rows, cols = grids(values.shape)
    rows = rows + first_row
    return jnp.where(rows > cols, values, jnp.where(rows == cols, F32(1.0), F32(0.0)))


def triangle_factor(values):
    rows, cols = grids(values.shape)
    scale = 2.0 / math.sqrt(values.shape[-1])
    return jnp.where(rows == cols, values, jnp.where(cols > rows, (values - 1.0) * scale, F32(0.0)))


def upper_part(values):
    rows, cols = grids(values.shape)
    return jnp.where(cols >= rows, values, F32(0.0))


def mix_level(leads, tree_v, tree_t, high, low):
    width = tree_v.shape[0]
    vees = upper_part(tree_v)
    tees = split(triangle_factor(tree_t).T)

    @pl.when(leads)
    def _():
        high[:, :width], low[:, :width] = tees
        high[:, width:], low[:, width:] = split(dot3(tees, split(vees.T)))

    @pl.when(jnp.logical_not(leads))
    def _():
        both = split(dot3(split(vees), tees))
        high[:, width:], low[:, width:] = both
        high[:, :width], low[:, :width] = split(dot3(both, split(vees.T)))


def start_all(pairs, sems):
    copies = [pltpu.make_async_copy(a, b, sems.at[i]) for i, (a, b) in enumerate(pairs)]
    for copy in copies:
        copy.start()
    return copies


def prepare_kernel(place, panel_t, tree_v, tree_t, trailing, th, tl, high, low, block, tri, vee, tee, sems):
    piece = trailing.at[:, : block.shape[1]]
    copies = start_all(((panel_t, tri), (tree_v.at[0], vee), (tree_t.at[0], tee), (piece, block)), sems)
    copies[0].wait()
    th[...], tl[...] = split(triangle_factor(tri[...]).T)
    copies[1].wait()
    copies[2].wait()
    mix_level(place[0] & 1 == 0, vee[...], tee[...], high, low)
    copies[3].wait()


def mixes_kernel(level, place, tree_v, tree_t, after, high, low):
    del after
    mix_level((place[0] >> level) & 1 == 0, tree_v[level], tree_t[level], high, low)


def opposite_rows(col, size, count):
    return pl.multiple_of(lax.rem(col + count // 2, count) * size, size)


def both_ways(rows, start):
    rows = unit_lower(rows, start)
    return split(rows), split(rows.T)


def early_kernel(place, own_a, own_b, behind_a, behind_b, before_a, before_b, block, partial, yh, yl, fh, fl):
    col = place[1]
    size = own_a.shape[0] + own_b.shape[0]
    count = block.shape[0] // size
    width = partial.shape[1]
    total = None
    behind = jnp.where(place[0] & 1 == 0, count - 1, 1)
    for shift, parts in ((0, (own_a, own_b)), (behind, (behind_a, behind_b)), (count - behind, (before_a, before_b))):
        start = pl.multiple_of(lax.rem(col + shift, count) * size, size)
        rows = jnp.concatenate([p[...] for p in parts], axis=0)
        here = pl.ds(start, size)
        straight, flipped = both_ways(rows, start)
        yh[here, :], yl[here, :] = straight
        fh[:, here], fl[:, here] = flipped
        term = dot3(flipped, split(block[pl.ds(start, size), :width]))
        total = term if total is None else total + term
    partial[...] = total


def store_parts(value, parts):
    first = 0
    for part in parts:
        part[...] = value[:, first : first + part.shape[1]]
        first += part.shape[1]


def first_kernel(place, partial, opp_a, opp_b, block, th, tl, yh, yl, *outs):
    tops, (proj, gh, gl, oh, ol, ph, plow) = outs[:-7], outs[-7:]
    size = opp_a.shape[0] + opp_b.shape[0]
    width = partial.shape[1]
    start = opposite_rows(place[1], size, block.shape[0] // size)
    rows = jnp.concatenate([opp_a[...], opp_b[...]], axis=0)
    straight, flipped = both_ways(rows, start)
    upper = [jnp.where(start == 0, new, old[:size, :]) for new, old in zip(straight, (yh, yl))]
    gain = split(dot3(upper, (th[...], tl[...])))
    value = partial[...] + dot3(flipped, split(block[pl.ds(start, size), :width]))
    store_parts(block[:size, :width] - dot3(gain, split(value)), tops)
    proj[...] = value
    gh[...], gl[...] = gain
    oh[...], ol[...] = straight
    ph[...], plow[...] = flipped


def assemble_kernel(place, yh_in, yl_in, fh_in, fl_in, oh, ol, ph, plow, yh, yl, fh, fl):
    size = oh.shape[0]
    here = pl.ds(opposite_rows(place[1], size, yh.shape[0] // size), size)
    for out, old, new in ((yh, yh_in, oh), (yl, yl_in, ol)):
        out[...] = old[...]
        out[here, :] = new[...]
    for out, old, new in ((fh, fh_in, ph), (fl, fl_in, plow)):
        out[...] = old[...]
        out[:, here] = new[...]


def next_kernel(span, block, fh, fl, gh, gl, top, proj):
    values = block[:, span]
    value = dot3((fh[...], fl[...]), split(values))
    top[...] = values[: top.shape[0]] - dot3((gh[...], gl[...]), split(value))
    proj[...] = value


def rest_kernel(first, block, yh, yl, th, tl, *args):
    projs, (out, slots, sems) = args[: -3 - (first > 0)], args[-3:]
    count, size, width = slots.shape
    weights = [split(dot3((th[...], tl[...]), split(proj[...]))) for proj in projs]
    copies = []
    for i in range(count):
        here = slice((i + 1) * size, (i + 2) * size)
        at = 0
        for weight in weights:
            wide = weight[0].shape[1]
            values = block[here, first + at : first + at + wide]
            slots[i, :, at : at + wide] = values - dot3((yh[here, :], yl[here, :]), weight)
            at += wide
        target = out.at[pl.ds((i + 1) * size, size), pl.ds(first, width)]
        copies.append(pltpu.make_async_copy(slots.at[i], target, sems.at[i]))
        copies[-1].start()
    for copy in copies:
        copy.wait()


def mixed(mine, theirs, high, low):
    width = mine.shape[0]
    one = dot3((high[:, :width], low[:, :width]), split(mine[...]))
    two = dot3((high[:, width:], low[:, width:]), split(theirs[...]))
    return mine[...] - (one + two)


def base_kernel(mine, high, low, base):
    width = mine.shape[0]
    base[...] = mine[...] - dot3((high[:, :width], low[:, :width]), split(mine[...]))


def level_kernel(mine, theirs, high, low, *parts):
    store_parts(mixed(mine, theirs, high, low), parts)


def final_kernel(first, count, high, low, *args):
    pieces, (out, slots, sems) = args[: 2 * count], args[-3:]
    half, w = slots.shape[2:]
    copies = []
    for k in range(count):
        mine, theirs = pieces[2 * k : 2 * k + 2]
        used = [theirs[...]] if count == 1 else [mine[...], theirs[...]]
        both = split(jnp.concatenate(used, axis=0))
        first_column = high.shape[1] - both[0].shape[0]
        for i in range(2):
            rows = slice(i * half, (i + 1) * half)
            slots[k, i] = mine[rows, :] - dot3((high[rows, first_column:], low[rows, first_column:]), both)
            target = out.at[pl.ds(i * half, half), pl.ds(first + k * w, w)]
            copies.append(pltpu.make_async_copy(slots.at[k, i], target, sems.at[k, i]))
            copies[-1].start()
    for copy in copies:
        copy.wait()


def shaped(shape, dtype=F32):
    return jax.ShapeDtypeStruct(shape, dtype)


def layout():
    units, chunks, first = [], [], 0
    for unit in UNITS:
        units.append((first, sum(unit)))
        for w in unit:
            chunks.append((first, w))
            first += w
    return units, chunks


def call(kernel, **options):
    mib = options.pop("mib")
    flops, moved = options.pop("cost")
    return pl.pallas_call(
        kernel,
        compiler_params=pltpu.CompilerParams(vmem_limit_bytes=mib << 20),
        cost_estimate=pl.CostEstimate(flops=flops, bytes_accessed=moved, transcendentals=0),
        **options,
    )


def fixed(values):
    return pltpu.with_memory_space_constraint(values, pltpu.HBM)


def update(trailing, panel_y, panel_t, tree_v, tree_t):
    size, width = panel_y.shape
    rows, columns = trailing.shape
    levels = tree_v.shape[0]
    count = lax.axis_size("col")
    place = jnp.stack([lax.axis_index("row"), lax.axis_index("col")]).astype(jnp.int32)
    own_a, own_b = panel_y[: size // 2], panel_y[size // 2 :]

    def ring(values, step):
        route = []
        for r in range(lax.axis_size("row")):
            for c in range(count):
                to = (c + (step if r % 2 == 0 else -step)) % count
                route.append((r * count + c, r * count + to))
        return lax.ppermute(values, ("row", "col"), route)

    behind_a = ring(own_a, 1)
    before_b = ring(own_b, -1)
    behind_b = ring(own_b, 1)
    before_a = ring(own_a, -1)
    opp_a = ring(behind_a, 1)
    opp_b = ring(before_b, -1)

    square = shaped((width, width), BF16)
    mix = shaped((width, 2 * width), BF16)
    tall = shaped((rows, width), BF16)
    wide = shaped((width, rows), BF16)
    cube = 2 * 3 * width**3
    units, chunks = layout()
    steps = [(units[step[0]][0], sum(units[u][1] for u in step)) for step in STEPS]
    w = steps[0][1]
    th, tl, *mixes, block = call(
        prepare_kernel,
        out_shape=[square, square, mix, mix, shaped((rows, w))],
        in_specs=[SMEM] + [HBM] * 4,
        out_specs=[VMEM] * 5,
        scratch_shapes=[pltpu.VMEM((width, width), F32)] * 3 + [pltpu.SemaphoreType.DMA((4,))],
        mib=8,
        cost=(3 * cube, 1 << 20),
    )(place, fixed(panel_t), fixed(tree_v), fixed(tree_t), fixed(trailing))

    partial, yh, yl, fh, fl = call(
        early_kernel,
        out_shape=[shaped((width, w)), tall, tall, wide, wide],
        in_specs=[SMEM] + [VMEM] * 7,
        out_specs=[VMEM] * 5,
        mib=16,
        cost=(2 * cube, 4 << 20),
    )(place, own_a, own_b, behind_a, behind_b, before_a, before_b, block)

    outs = call(
        first_kernel,
        out_shape=[shaped((width, units[u][1])) for u in STEPS[0]] + [shaped((width, w))] + [square] * 6,
        in_specs=[SMEM] + [VMEM] * 8,
        out_specs=[VMEM] * (7 + len(STEPS[0])),
        mib=16,
        cost=(2 * cube, 2 << 20),
    )(place, partial, opp_a, opp_b, block, th, tl, yh, yl)
    raw, (proj, gh, gl, *opposite) = list(outs[:-7]), outs[-7:]
    projs = [proj]

    yh, yl, fh, fl = call(
        assemble_kernel,
        out_shape=[tall, tall, wide, wide],
        in_specs=[SMEM] + [VMEM] * 8,
        out_specs=[VMEM] * 4,
        mib=16,
        cost=(0, 4 << 20),
    )(place, yh, yl, fh, fl, *opposite)

    def swap(level, values):
        route = [(r, r ^ (1 << level)) for r in range(lax.axis_size("row"))]
        return lax.ppermute(values, "row", route)

    def base_of(level, values):
        return call(
            base_kernel,
            out_shape=shaped(values.shape),
            in_specs=[VMEM] * 3,
            out_specs=VMEM,
            mib=8,
            cost=(cube * values.shape[1] // width, 1 << 19),
        )(values, *mixes[2 * level : 2 * level + 2])

    def combine(level, values, widths):
        w = values.shape[1]
        return call(
            level_kernel,
            out_shape=[shaped((width, w)) for w in widths],
            in_specs=[VMEM] * 4,
            out_specs=[VMEM] * len(widths),
            mib=8,
            cost=(2 * cube * w // width, 1 << 20),
        )(values, swap(level, values), *mixes[2 * level : 2 * level + 2])

    def mix_matrices(level, after):
        mixes.extend(
            call(
                functools.partial(mixes_kernel, level),
                out_shape=[mix] * 2,
                in_specs=[SMEM] + [VMEM] * 2 + [ANY],
                out_specs=[VMEM] * 2,
                mib=8,
                cost=(2 * cube, 1 << 20),
            )(place, tree_v, tree_t, after)
        )

    for k, (first, w) in enumerate(steps):
        if k:
            top, proj = call(
                functools.partial(next_kernel, slice(first, first + w)),
                out_shape=[shaped((width, w))] * 2,
                in_specs=[VMEM] * 5,
                out_specs=[VMEM] * 2,
                mib=16,
                cost=(5 * cube * w // width, 2 << 20),
            )(trailing, fh, fl, gh, gl)
            raw.append(top)
            projs.append(proj)
    for level in range(1, levels):
        mix_matrices(level, projs[0] if level < levels - 1 else projs[-1])
    tops = []
    for u, top in enumerate(raw):
        tops += combine(0, top, UNITS[u])

    for level in range(1, levels - 1):
        tops = [combine(level, top, (top.shape[1],))[0] for top in tops]

    level = levels - 1
    out = ()
    parts = rows // size - 1
    for group in ((0, 1), (2, 3)):
        first = steps[group[0]][0]
        w = sum(steps[k][1] for k in group)
        out = (
            call(
                functools.partial(rest_kernel, first),
                out_shape=shaped((rows, columns)),
                in_specs=[VMEM] * (5 + len(group)) + [HBM] * len(out),
                out_specs=HBM,
                scratch_shapes=[pltpu.VMEM((parts, size, w), F32), pltpu.SemaphoreType.DMA((parts,))],
                input_output_aliases={5 + len(group): 0} if out else {},
                mib=16,
                cost=(10 * cube, 4 << 20),
            )(trailing, yh, yl, th, tl, *[projs[k] for k in group], *out),
        )
    out = out[0]

    for group in ENDS:
        first, w = chunks[group[0]]
        n = len(group)
        pieces = []
        for k in group:
            pieces += [base_of(level, tops[k]) if n == 1 else tops[k], swap(level, tops[k])]
        out = call(
            functools.partial(final_kernel, first, n),
            out_shape=shaped((rows, columns)),
            in_specs=[VMEM] * (2 + 2 * n) + [HBM],
            out_specs=HBM,
            scratch_shapes=[pltpu.VMEM((n, 2, width // 2, w), F32), pltpu.SemaphoreType.DMA((n, 2))],
            input_output_aliases={2 + 2 * n: 0},
            mib=8,
            cost=(2 * cube * n * w // width, 1 << 20),
        )(*mixes[2 * level :], *pieces, out)
    return out


def solution(mesh):
    placed = (
        P("row", "col"),
        P(("row", "col"), None),
        P("row", None),
        P(None, "row", None),
        P(None, "row", None),
    )
    return jax.shard_map(update, mesh=mesh, in_specs=placed, out_specs=P("row", "col"), check_vma=False)
```
